256 devices in a mesh: seq: 32 (over x_lo, z, core), tp: 8 (over y, x_hi).
Axes of the slice: x: 4 (x_hi: 2, x_lo: 2; x = x_hi * 2 + x_lo), y: 4, z: 8, core: 2. Of those that a mesh axis runs over, the one named last changes fastest.
Arguments:
- values: bfloat16 [8192, 4096], P('seq', 'tp'), may hold values from -6 to 6
- gate: bfloat16 [8192, 4096], P('seq', 'tp'), may hold values from -6 to 6
- out_grad: bfloat16 [8192, 4096], P('seq', 'tp'), may hold values from -6 to 6
- out_weight: bfloat16 [4096, 4096], P(None, 'tp'), may hold values from -0.09375 to 0.09375
- filt: float32 [8192, 4096], P('seq', 'tp'), may hold values from -6 to 6
- decay: float32 [4096], P('tp'), may hold values from 0.5 to 16
Outputs:
- d_values: bfloat16 [8192, 4096], P('seq', 'tp')
- d_gate: bfloat16 [8192, 4096], P('seq', 'tp')
- d_filt: float32 [8192, 4096], P('seq', 'tp')
- decay_grad: float32 [4096], P('tp')
- d_out_weight: float32 [4096, 4096], P('seq', 'tp')
The draws below stay inside these ranges and needn't reach their ends.
All inputs are finite; a program needn't handle non-finite values.
Results may differ from the reference program's by a relative error of at most 0.0085.
Values may be sent and summed in bfloat16 or wider, within the bound.
A program may use at most 128 MiB of HBM per device.

```python
import math
import jax
import jax.numpy as jnp
from jax import lax

D = 4096
TOKENS = 8192


def with_spikes(values, rng, source, target, shards_of, factor):
    def block_of(axis_at):
        return (jnp.arange(values.shape[axis_at]) // (values.shape[axis_at] // shards_of)).reshape((-1,) + (1,) * (values.ndim - 1 - axis_at))

    first = jax.random.permutation(rng, shards_of)[block_of(target)]
    other_side = (block_of(target) + shards_of // 2) % shards_of
    return jnp.where((block_of(source) == first) | (block_of(source) == other_side), factor * values, values)


def block_levels(rng, dims, shards, least, largest):
    level = 1.0
    for dim, shards_of in shards:
        heights = jax.random.uniform(jax.random.fold_in(jax.random.fold_in(rng, 6), dim), (shards_of,), jnp.float32, least / len(shards), largest / len(shards))
        level = level * jnp.repeat(jnp.exp(heights), dims[dim] // shards_of).reshape((-1,) + (1,) * (len(dims) - 1 - dim))
    return level


def centred(rng, dims, scale, bound, pieces=(), kind=jnp.bfloat16):
    factor_of = block_levels(rng, dims, pieces, -0.22, 0.18) if pieces else 1.0
    drawn = jax.random.normal(rng, dims, jnp.float32) * scale * factor_of
    return jnp.minimum(jnp.maximum(drawn, -bound), bound).astype(kind)


def noise_with(key, dims, spread, most, shards, heavy, kind=jnp.bfloat16):
    drawn = spread * jax.random.normal(key, dims, jnp.float32)
    if shards:
        drawn = drawn * block_levels(key, dims, shards, -0.22, 0.18)
    return jnp.clip(with_spikes(drawn, jax.random.fold_in(key, 3), *heavy), -most, most).astype(kind)


def setup_inputs(seed: int = 0) -> dict:
    seeds = jax.random.split(jax.random.key(seed), 7)
    return {
        "values": centred(seeds[0], (TOKENS, D), 1.0, 6.0, ((0, 32), (1, 8))),
        "gate": centred(seeds[1], (TOKENS, D), 1.0, 6.0, ((0, 32), (1, 8))),
        "out_grad": noise_with(seeds[2], (TOKENS, D), 1.0, 6.0, ((0, 32), (1, 8)), (0, 1, 32, 2.75)),
        "out_weight": centred(seeds[3], (D, D), D ** -0.5, 0.09375, ((1, 8),)),
        "filt": centred(seeds[4], (TOKENS, D), 1.0, 6.0, ((0, 32), (1, 8)), jnp.float32),
        "decay": jnp.clip(jnp.exp(math.log(16.0) - 3.465736 * jax.random.uniform(seeds[5], (D,), jnp.float32) ** block_levels(seeds[5], (D,), ((0, 8),), -0.2, 0.2)), 0.5, 16.0),
    }


def conv_block(inputs):
    values_blk, kernel_blk, grad_blk = inputs
    count = values_blk.shape[0]
    padded = 2 * count
    spec_v = jnp.fft.rfft(values_blk, n=padded, axis=0)
    spec_k = jnp.fft.rfft(kernel_blk, n=padded, axis=0)
    spec_g = jnp.fft.rfft(grad_blk, n=padded, axis=0)
    conv_out = jnp.fft.irfft(spec_v * spec_k, n=padded, axis=0)[:count]
    conv_grad = jnp.fft.irfft(jnp.conj(spec_k) * spec_g, n=padded, axis=0)[:count]
    kernel_grad = jnp.fft.irfft(jnp.conj(spec_v) * spec_g, n=padded, axis=0)[:count]
    return (conv_out, conv_grad, kernel_grad)

def reference(values, gate, out_grad, out_weight, filt, decay):
    grad_y = jnp.dot(out_grad, out_weight, preferred_element_type=jnp.float32).astype(jnp.bfloat16)
    position = (jnp.arange(TOKENS, dtype=jnp.int32).astype(jnp.float32) / TOKENS)[:, None]
    norm_scale = 1.0 / math.sqrt(TOKENS)
    window = jnp.exp(-decay[None, :] * position)
    kernel = filt * window * norm_scale
    gated_grad = grad_y.astype(jnp.float32) * gate.astype(jnp.float32)
    block_width = math.gcd(D, 512)
    blocks = D // block_width

    def split_up(array):
        return array.reshape(TOKENS, blocks, block_width).transpose(1, 0, 2)

    def join_up(array):
        return array.transpose(1, 0, 2).reshape(TOKENS, D)
    conv_out, conv_grad, kernel_grad = lax.map(conv_block, (split_up(values.astype(jnp.float32)), split_up(kernel), split_up(gated_grad)))
    conv_out = join_up(conv_out)
    conv_grad = join_up(conv_grad)
    kernel_grad = join_up(kernel_grad)
    d_values = conv_grad.astype(jnp.bfloat16)
    d_gate = (grad_y.astype(jnp.float32) * conv_out).astype(jnp.bfloat16)
    d_filt = kernel_grad * window * norm_scale
    decay_grad = -norm_scale * lax.optimization_barrier(jnp.sum(position * kernel_grad * kernel, axis=0))
    gated_out = (gate.astype(jnp.float32) * conv_out).astype(jnp.bfloat16)
    d_out_weight = jnp.dot(out_grad.T, gated_out, preferred_element_type=jnp.float32) * norm_scale
    return (d_values, d_gate, d_filt, decay_grad, d_out_weight)
```

```python
import math

import jax
import jax.numpy as jnp
from jax import lax
from jax.sharding import PartitionSpec as P


def to_channels(block, parts):
    lead = block.shape[:-2]
    tok_rows, width = block.shape[-2:]
    sub = width // parts
    nd = len(lead)
    split = block.reshape(lead + (tok_rows, parts, sub))
    perm = tuple(range(nd)) + (nd + 1, nd + 2, nd)
    split = jnp.transpose(split, perm)
    moved = lax.all_to_all(split, "seq", split_axis=nd, concat_axis=nd, tiled=True)
    perm = tuple(range(nd)) + (nd + 1, nd, nd + 2)
    moved = jnp.transpose(moved, perm)
    return moved.reshape(lead + (sub, parts * tok_rows))


def to_tokens(block, parts):
    lead = block.shape[:-2]
    sub, length = block.shape[-2:]
    tok_rows = length // parts
    nd = len(lead)
    split = block.reshape(lead + (sub, parts, tok_rows))
    perm = tuple(range(nd)) + (nd + 1, nd, nd + 2)
    split = jnp.transpose(split, perm)
    moved = lax.all_to_all(split, "seq", split_axis=nd, concat_axis=nd, tiled=True)
    moved = moved.reshape(lead + (parts * sub, tok_rows))
    perm = tuple(range(nd)) + (nd + 1, nd)
    return jnp.transpose(moved, perm)


def on_device(values, gate, out_grad, out_weight, filt, decay):
    tok_rows, width = values.shape
    parts = lax.axis_size("seq")
    my_index = lax.axis_index("seq")
    sub = width // parts
    length = tok_rows * parts
    padded = 2 * length
    norm_scale = 1.0 / math.sqrt(length)

    full_grad = lax.all_gather(out_grad, "tp", axis=1, tiled=True)
    grad_y = jnp.dot(full_grad, out_weight, preferred_element_type=jnp.float32).astype(jnp.bfloat16)

    halves = to_channels(jnp.stack([values, gate, grad_y]), parts)
    filt_c = to_channels(filt, parts)
    values_c = halves[0].astype(jnp.float32)
    gate_c = halves[1].astype(jnp.float32)
    grad_c = halves[2].astype(jnp.float32)

    my_decay = lax.dynamic_slice_in_dim(decay, my_index * sub, sub)
    position = (jnp.arange(length, dtype=jnp.int32).astype(jnp.float32) / length)[None, :]
    window = jnp.exp(-my_decay[:, None] * position)
    kernel = filt_c * window * norm_scale
    gated_grad = grad_c * gate_c

    spec_v = jnp.fft.rfft(values_c, n=padded, axis=-1)
    spec_k = jnp.fft.rfft(kernel, n=padded, axis=-1)
    spec_g = jnp.fft.rfft(gated_grad, n=padded, axis=-1)
    conv_out = jnp.fft.irfft(spec_v * spec_k, n=padded, axis=-1)[:, :length]
    conv_grad = jnp.fft.irfft(jnp.conj(spec_k) * spec_g, n=padded, axis=-1)[:, :length]
    kernel_grad = jnp.fft.irfft(jnp.conj(spec_v) * spec_g, n=padded, axis=-1)[:, :length]

    d_values = conv_grad.astype(jnp.bfloat16)
    d_gate = (grad_c * conv_out).astype(jnp.bfloat16)
    gated_out = (gate_c * conv_out).astype(jnp.bfloat16)
    d_filt_c = kernel_grad * window * norm_scale
    decay_part = jnp.sum(position * kernel_grad * kernel, axis=1)

    back = to_tokens(jnp.stack([d_values, d_gate, gated_out]), parts)
    d_filt = to_tokens(d_filt_c, parts)
    decay_grad = -norm_scale * lax.all_gather(decay_part, "seq", axis=0, tiled=True)

    term = lax.dot_general(
        full_grad, back[2], (((0,), (0,)), ((), ())), preferred_element_type=jnp.float32
    )
    d_out_weight = lax.psum_scatter(term * norm_scale, "seq", scatter_dimension=0, tiled=True)
    return (back[0], back[1], d_filt, decay_grad, d_out_weight)


def solution(mesh):
    in_specs = (
        P("seq", "tp"),
        P("seq", "tp"),
        P("seq", "tp"),
        P(None, "tp"),
        P("seq", "tp"),
        P("tp"),
    )
    out_specs = (P("seq", "tp"), P("seq", "tp"), P("seq", "tp"), P("tp"), P("seq", "tp"))
    return jax.shard_map(
        on_device, mesh=mesh, in_specs=in_specs, out_specs=out_specs, check_vma=False
    )
```

```python
import math

import jax
import jax.numpy as jnp
from jax import lax
from jax.sharding import PartitionSpec as P

HIGHEST = lax.Precision.HIGHEST
TWO_PI = 2.0 * math.pi


def angles(left, right, modulus):
    index = left[:, None] * right[None, :] % modulus
    phase = index.astype(jnp.float32) * (TWO_PI / modulus)
    return jnp.cos(phase), jnp.sin(phase)


def to_channels(block, parts):
    lead = block.shape[:-2]
    tok_rows, width = block.shape[-2:]
    nd = len(lead)
    split = block.reshape(lead + (tok_rows, parts, width // parts))
    split = jnp.transpose(split, tuple(range(nd)) + (nd + 1, nd + 2, nd))
    return lax.all_to_all(split, "seq", split_axis=nd, concat_axis=nd, tiled=True)


def to_tokens(block, parts):
    lead = block.shape[:-3]
    _, sub, tok_rows = block.shape[-3:]
    nd = len(lead)
    moved = lax.all_to_all(block, "seq", split_axis=nd, concat_axis=nd, tiled=True)
    moved = moved.reshape(lead + (parts * sub, tok_rows))
    return jnp.transpose(moved, tuple(range(nd)) + (nd + 1, nd))


class Dft:
    def __init__(self, parts, rows):
        outer = 2 * parts
        self.n = outer * rows
        self.rows = rows
        p_idx = jnp.arange(parts, dtype=jnp.int32)
        k1_idx = jnp.arange(outer, dtype=jnp.int32)
        r_idx = jnp.arange(rows, dtype=jnp.int32)
        c1, s1 = angles(k1_idx, p_idx, outer)
        self.fwd_outer = jnp.concatenate([c1, -s1], axis=0)
        self.inv_outer = jnp.concatenate([c1.T, -s1.T], axis=1) / self.n
        self.twid_c, self.twid_s = angles(k1_idx, r_idx, self.n)
        gc, gs = angles(r_idx, r_idx, rows)
        self.fwd_inner = jnp.concatenate(
            [jnp.concatenate([gc, -gs], axis=1), jnp.concatenate([gs, gc], axis=1)], axis=0
        )
        self.inv_inner = jnp.concatenate(
            [jnp.concatenate([gc, gs], axis=1), jnp.concatenate([-gs, gc], axis=1)], axis=0
        )

    def forward(self, x):
        y = jnp.einsum("kp,fpcr->fkcr", self.fwd_outer, x, precision=HIGHEST)
        outer = self.fwd_outer.shape[0] // 2
        yr, yi = y[:, :outer], y[:, outer:]
        tc = self.twid_c[None, :, None, :]
        ts = self.twid_s[None, :, None, :]
        zr = yr * tc + yi * ts
        zi = yi * tc - yr * ts
        z = jnp.concatenate([zr, zi], axis=-1)
        out = jnp.einsum("fkcr,rq->fkcq", z, self.fwd_inner, precision=HIGHEST)
        return out[..., : self.rows], out[..., self.rows :]

    def inverse_real(self, zr, zi):
        z = jnp.concatenate([zr, zi], axis=-1)
        u = jnp.einsum("fkcq,qr->fkcr", z, self.inv_inner, precision=HIGHEST)
        ur, ui = u[..., : self.rows], u[..., self.rows :]
        tc = self.twid_c[None, :, None, :]
        ts = self.twid_s[None, :, None, :]
        vr = ur * tc - ui * ts
        vi = ur * ts + ui * tc
        v = jnp.concatenate([vr, vi], axis=1)
        return jnp.einsum("pk,fkcr->fpcr", self.inv_outer, v, precision=HIGHEST)


def on_device(values, gate, out_grad, out_weight, filt, decay):
    tok_rows, width = values.shape
    parts = lax.axis_size("seq")
    my_index = lax.axis_index("seq")
    sub = width // parts
    length = tok_rows * parts
    norm_scale = 1.0 / math.sqrt(length)

    early = to_channels(jnp.stack([values, gate]), parts)
    filt_c = to_channels(filt, parts)

    full_grad = lax.all_gather(out_grad, "tp", axis=1, tiled=True)
    grad_y = jnp.dot(full_grad, out_weight, preferred_element_type=jnp.float32).astype(jnp.bfloat16)
    grad_c = to_channels(grad_y, parts).astype(jnp.float32)

    values_c = early[0].astype(jnp.float32)
    gate_c = early[1].astype(jnp.float32)

    my_decay = lax.dynamic_slice_in_dim(decay, my_index * sub, sub)
    tok = (
        jnp.arange(parts, dtype=jnp.int32)[:, None, None] * tok_rows
        + jnp.arange(tok_rows, dtype=jnp.int32)[None, None, :]
    )
    position = tok.astype(jnp.float32) / length
    window = jnp.exp(-my_decay[None, :, None] * position)
    kernel = filt_c * window * norm_scale
    gated_grad = grad_c * gate_c

    dft = Dft(parts, tok_rows)
    vk_r, vk_i = dft.forward(jnp.stack([values_c, kernel]))
    g_r, g_i = dft.forward(gated_grad[None])
    v_r, k_r = vk_r[0], vk_r[1]
    v_i, k_i = vk_i[0], vk_i[1]
    g_r, g_i = g_r[0], g_i[0]
    prod_r = jnp.stack([v_r * k_r - v_i * k_i, k_r * g_r + k_i * g_i, v_r * g_r + v_i * g_i])
    prod_i = jnp.stack([v_r * k_i + v_i * k_r, k_r * g_i - k_i * g_r, v_r * g_i - v_i * g_r])
    conv = dft.inverse_real(prod_r, prod_i)
    conv_out, conv_grad, kernel_grad = conv[0], conv[1], conv[2]

    d_values = conv_grad.astype(jnp.bfloat16)
    d_gate = (grad_c * conv_out).astype(jnp.bfloat16)
    gated_out = (gate_c * conv_out).astype(jnp.bfloat16)
    d_filt_c = kernel_grad * window * norm_scale
    decay_part = jnp.sum(position * kernel_grad * kernel, axis=(0, 2))

    back = to_tokens(jnp.stack([d_values, d_gate, gated_out]), parts)
    d_filt = to_tokens(d_filt_c, parts)
    spread = jnp.broadcast_to(decay_part[None, :], (parts, sub))
    gathered = lax.all_to_all(spread, "seq", split_axis=0, concat_axis=0, tiled=True)
    decay_grad = -norm_scale * gathered.reshape(width)

    term = lax.dot_general(
        full_grad, back[2], (((0,), (0,)), ((), ())), preferred_element_type=jnp.float32
    )
    d_out_weight = lax.psum_scatter(term * norm_scale, "seq", scatter_dimension=0, tiled=True)
    return (back[0], back[1], d_filt, decay_grad, d_out_weight)


def solution(mesh):
    in_specs = (
        P("seq", "tp"),
        P("seq", "tp"),
        P("seq", "tp"),
        P(None, "tp"),
        P("seq", "tp"),
        P("tp"),
    )
    out_specs = (P("seq", "tp"), P("seq", "tp"), P("seq", "tp"), P("tp"), P("seq", "tp"))
    return jax.shard_map(
        on_device, mesh=mesh, in_specs=in_specs, out_specs=out_specs, check_vma=False
    )
```

```python
import math

import jax
import jax.numpy as jnp
from jax import lax
from jax.sharding import PartitionSpec as P

HIGHEST = lax.Precision.HIGHEST
TWO_PI = 2.0 * math.pi


def angles(left, right, modulus):
    index = left[:, None] * right[None, :] % modulus
    phase = index.astype(jnp.float32) * (TWO_PI / modulus)
    return jnp.cos(phase), jnp.sin(phase)


def to_channels(block, parts):
    lead = block.shape[:-2]
    tok_rows, width = block.shape[-2:]
    nd = len(lead)
    split = block.reshape(lead + (tok_rows, parts, width // parts))
    split = jnp.transpose(split, tuple(range(nd)) + (nd + 1, nd + 2, nd))
    return lax.all_to_all(split, "seq", split_axis=nd, concat_axis=nd, tiled=True)


def to_tokens(block, parts):
    lead = block.shape[:-3]
    _, sub, tok_rows = block.shape[-3:]
    nd = len(lead)
    moved = lax.all_to_all(block, "seq", split_axis=nd, concat_axis=nd, tiled=True)
    moved = moved.reshape(lead + (parts * sub, tok_rows))
    return jnp.transpose(moved, tuple(range(nd)) + (nd + 1, nd))


class Dft:
    def __init__(self, parts, rows):
        outer = 2 * parts
        self.n = outer * rows
        self.rows = rows
        p_idx = jnp.arange(parts, dtype=jnp.int32)
        k1_idx = jnp.arange(outer, dtype=jnp.int32)
        r_idx = jnp.arange(rows, dtype=jnp.int32)
        c1, s1 = angles(k1_idx, p_idx, outer)
        self.fwd_outer = jnp.concatenate([c1, -s1], axis=0)
        self.inv_outer = jnp.concatenate([c1.T, -s1.T], axis=1) / self.n
        self.twid_c, self.twid_s = angles(k1_idx, r_idx, self.n)
        gc, gs = angles(r_idx, r_idx, rows)
        self.fwd_inner = jnp.concatenate(
            [jnp.concatenate([gc, -gs], axis=1), jnp.concatenate([gs, gc], axis=1)], axis=0
        )
        self.inv_inner = jnp.concatenate(
            [jnp.concatenate([gc, gs], axis=1), jnp.concatenate([-gs, gc], axis=1)], axis=0
        )

    def forward(self, x):
        y = jnp.einsum("kp,fpcr->fkcr", self.fwd_outer, x, precision=HIGHEST)
        outer = self.fwd_outer.shape[0] // 2
        yr, yi = y[:, :outer], y[:, outer:]
        tc = self.twid_c[None, :, None, :]
        ts = self.twid_s[None, :, None, :]
        zr = yr * tc + yi * ts
        zi = yi * tc - yr * ts
        z = jnp.concatenate([zr, zi], axis=-1)
        out = jnp.einsum("fkcr,rq->fkcq", z, self.fwd_inner, precision=HIGHEST)
        return out[..., : self.rows], out[..., self.rows :]

    def inverse_real(self, zr, zi):
        z = jnp.concatenate([zr, zi], axis=-1)
        u = jnp.einsum("fkcq,qr->fkcr", z, self.inv_inner, precision=HIGHEST)
        ur, ui = u[..., : self.rows], u[..., self.rows :]
        tc = self.twid_c[None, :, None, :]
        ts = self.twid_s[None, :, None, :]
        vr = ur * tc - ui * ts
        vi = ur * ts + ui * tc
        v = jnp.concatenate([vr, vi], axis=1)
        return jnp.einsum("pk,fkcr->fpcr", self.inv_outer, v, precision=HIGHEST)


def on_device(values, gate, out_grad, out_weight, filt, decay):
    tok_rows, width = values.shape
    parts = lax.axis_size("seq")
    my_index = lax.axis_index("seq")
    sub = width // parts
    length = tok_rows * parts
    norm_scale = 1.0 / math.sqrt(length)

    early = to_channels(jnp.stack([values, gate]), parts)
    filt_c = to_channels(filt, parts)

    full_grad = lax.all_gather(out_grad, "tp", axis=1, tiled=True)
    grad_y = jnp.dot(full_grad, out_weight, preferred_element_type=jnp.float32).astype(jnp.bfloat16)
    grad_c = to_channels(grad_y, parts).astype(jnp.float32)

    values_c = early[0].astype(jnp.float32)
    gate_c = early[1].astype(jnp.float32)

    my_decay = lax.dynamic_slice_in_dim(decay, my_index * sub, sub)
    tok = (
        jnp.arange(parts, dtype=jnp.int32)[:, None, None] * tok_rows
        + jnp.arange(tok_rows, dtype=jnp.int32)[None, None, :]
    )
    position = tok.astype(jnp.float32) / length
    window = jnp.exp(-my_decay[None, :, None] * position)
    kernel = filt_c * window * norm_scale
    gated_grad = grad_c * gate_c

    dft = Dft(parts, tok_rows)
    vk_r, vk_i = dft.forward(jnp.stack([values_c, kernel]))
    g_r, g_i = dft.forward(gated_grad[None])
    v_r, k_r = vk_r[0], vk_r[1]
    v_i, k_i = vk_i[0], vk_i[1]
    g_r, g_i = g_r[0], g_i[0]
    prod_r = jnp.stack([v_r * k_r - v_i * k_i, k_r * g_r + k_i * g_i, v_r * g_r + v_i * g_i])
    prod_i = jnp.stack([v_r * k_i + v_i * k_r, k_r * g_i - k_i * g_r, v_r * g_i - v_i * g_r])
    conv = dft.inverse_real(prod_r, prod_i)
    conv_out, conv_grad, kernel_grad = conv[0], conv[1], conv[2]

    d_values = conv_grad.astype(jnp.bfloat16)
    d_gate = (grad_c * conv_out).astype(jnp.bfloat16)
    gated_out = (gate_c * conv_out).astype(jnp.bfloat16)
    d_filt_c = kernel_grad * window * norm_scale
    decay_part = jnp.sum(position * kernel_grad * kernel, axis=(0, 2))

    gated_home = to_tokens(gated_out, parts)
    term = lax.dot_general(
        full_grad, gated_home, (((0,), (0,)), ((), ())), preferred_element_type=jnp.float32
    )
    features = term.shape[0]
    pieces = (term * norm_scale).astype(jnp.bfloat16).reshape(parts, features // parts, width)
    pieces = lax.all_to_all(pieces, "seq", split_axis=0, concat_axis=0, tiled=True)
    d_out_weight = jnp.sum(pieces.astype(jnp.float32), axis=0)

    back = to_tokens(jnp.stack([d_values, d_gate]), parts)
    d_filt = to_tokens(d_filt_c, parts)
    spread = jnp.broadcast_to(decay_part[None, :], (parts, sub))
    gathered = lax.all_to_all(spread, "seq", split_axis=0, concat_axis=0, tiled=True)
    decay_grad = -norm_scale * gathered.reshape(width)
    return (back[0], back[1], d_filt, decay_grad, d_out_weight)


def solution(mesh):
    in_specs = (
        P("seq", "tp"),
        P("seq", "tp"),
        P("seq", "tp"),
        P(None, "tp"),
        P("seq", "tp"),
        P("tp"),
    )
    out_specs = (P("seq", "tp"), P("seq", "tp"), P("seq", "tp"), P("tp"), P("seq", "tp"))
    return jax.shard_map(
        on_device, mesh=mesh, in_specs=in_specs, out_specs=out_specs, check_vma=False
    )
```

```python
import math

import jax
import jax.numpy as jnp
from jax import lax
from jax.sharding import PartitionSpec as P

HIGHEST = lax.Precision.HIGHEST
TWO_PI = 2.0 * math.pi


def angles(left, right, modulus):
    index = left[:, None] * right[None, :] % modulus
    phase = index.astype(jnp.float32) * (TWO_PI / modulus)
    return jnp.cos(phase), jnp.sin(phase)


def to_channels(block, parts):
    lead = block.shape[:-2]
    tok_rows, width = block.shape[-2:]
    nd = len(lead)
    split = block.reshape(lead + (tok_rows, parts, width // parts))
    split = jnp.transpose(split, tuple(range(nd)) + (nd + 1, nd + 2, nd))
    return lax.all_to_all(split, "seq", split_axis=nd, concat_axis=nd, tiled=True)


def to_tokens(block, parts):
    lead = block.shape[:-3]
    _, sub, tok_rows = block.shape[-3:]
    nd = len(lead)
    moved = lax.all_to_all(block, "seq", split_axis=nd, concat_axis=nd, tiled=True)
    moved = moved.reshape(lead + (parts * sub, tok_rows))
    return jnp.transpose(moved, tuple(range(nd)) + (nd + 1, nd))


class Dft:
    def __init__(self, parts, rows):
        outer = 2 * parts
        self.n = outer * rows
        self.rows = rows
        p_idx = jnp.arange(parts, dtype=jnp.int32)
        k1_idx = jnp.arange(outer, dtype=jnp.int32)
        r_idx = jnp.arange(rows, dtype=jnp.int32)
        c1, s1 = angles(k1_idx, p_idx, outer)
        self.fwd_outer = jnp.concatenate([c1, -s1], axis=0)
        self.inv_outer = jnp.concatenate([c1.T, -s1.T], axis=1) / self.n
        self.twid_c, self.twid_s = angles(k1_idx, r_idx, self.n)
        gc, gs = angles(r_idx, r_idx, rows)
        self.fwd_inner = jnp.concatenate(
            [jnp.concatenate([gc, -gs], axis=1), jnp.concatenate([gs, gc], axis=1)], axis=0
        )
        self.inv_inner = jnp.concatenate(
            [jnp.concatenate([gc, gs], axis=1), jnp.concatenate([-gs, gc], axis=1)], axis=0
        )

    def forward(self, x):
        y = jnp.einsum("kp,fpcr->fkcr", self.fwd_outer, x, precision=HIGHEST)
        outer = self.fwd_outer.shape[0] // 2
        yr, yi = y[:, :outer], y[:, outer:]
        tc = self.twid_c[None, :, None, :]
        ts = self.twid_s[None, :, None, :]
        zr = yr * tc + yi * ts
        zi = yi * tc - yr * ts
        z = jnp.concatenate([zr, zi], axis=-1)
        out = jnp.einsum("fkcr,rq->fkcq", z, self.fwd_inner, precision=HIGHEST)
        return out[..., : self.rows], out[..., self.rows :]

    def inverse_real(self, zr, zi):
        z = jnp.concatenate([zr, zi], axis=-1)
        u = jnp.einsum("fkcq,qr->fkcr", z, self.inv_inner, precision=HIGHEST)
        ur, ui = u[..., : self.rows], u[..., self.rows :]
        tc = self.twid_c[None, :, None, :]
        ts = self.twid_s[None, :, None, :]
        vr = ur * tc - ui * ts
        vi = ur * ts + ui * tc
        v = jnp.concatenate([vr, vi], axis=1)
        return jnp.einsum("pk,fkcr->fpcr", self.inv_outer, v, precision=HIGHEST)


def on_device(values, gate, out_grad, out_weight, filt, decay):
    tok_rows, width = values.shape
    parts = lax.axis_size("seq")
    my_index = lax.axis_index("seq")
    sub = width // parts
    length = tok_rows * parts
    norm_scale = 1.0 / math.sqrt(length)

    early = to_channels(jnp.stack([values, gate]), parts)
    filt_c = to_channels(filt, parts)

    full_grad = lax.all_gather(out_grad, "tp", axis=1, tiled=True)
    grad_y = jnp.dot(full_grad, out_weight, preferred_element_type=jnp.float32).astype(jnp.bfloat16)

    values_c = early[0].astype(jnp.float32)
    gate_c = early[1].astype(jnp.float32)

    my_decay = lax.dynamic_slice_in_dim(decay, my_index * sub, sub)
    tok = (
        jnp.arange(parts, dtype=jnp.int32)[:, None, None] * tok_rows
        + jnp.arange(tok_rows, dtype=jnp.int32)[None, None, :]
    )
    position = tok.astype(jnp.float32) / length
    window = jnp.exp(-my_decay[None, :, None] * position)
    kernel = filt_c * window * norm_scale

    dft = Dft(parts, tok_rows)
    vk_r, vk_i = dft.forward(jnp.stack([values_c, kernel]))
    v_r, k_r = vk_r[0], vk_r[1]
    v_i, k_i = vk_i[0], vk_i[1]
    conv_out = dft.inverse_real((v_r * k_r - v_i * k_i)[None], (v_r * k_i + v_i * k_r)[None])[0]
    gated_out = (gate_c * conv_out).astype(jnp.bfloat16)
    gated_home = to_tokens(gated_out, parts)
    term = lax.dot_general(
        full_grad, gated_home, (((0,), (0,)), ((), ())), preferred_element_type=jnp.float32
    )
    d_out_weight = lax.psum_scatter(term * norm_scale, "seq", scatter_dimension=0, tiled=True)

    grad_c = to_channels(grad_y, parts).astype(jnp.float32)
    gated_grad = grad_c * gate_c
    g_r, g_i = dft.forward(gated_grad[None])
    g_r, g_i = g_r[0], g_i[0]
    prod_r = jnp.stack([k_r * g_r + k_i * g_i, v_r * g_r + v_i * g_i])
    prod_i = jnp.stack([k_r * g_i - k_i * g_r, v_r * g_i - v_i * g_r])
    conv = dft.inverse_real(prod_r, prod_i)
    conv_grad, kernel_grad = conv[0], conv[1]

    d_values = conv_grad.astype(jnp.bfloat16)
    d_gate = (grad_c * conv_out).astype(jnp.bfloat16)
    d_filt_c = kernel_grad * window * norm_scale
    decay_part = jnp.sum(position * kernel_grad * kernel, axis=(0, 2))

    back = to_tokens(jnp.stack([d_values, d_gate]), parts)
    d_filt = to_tokens(d_filt_c, parts)
    spread = jnp.broadcast_to(decay_part[None, :], (parts, sub))
    gathered = lax.all_to_all(spread, "seq", split_axis=0, concat_axis=0, tiled=True)
    decay_grad = -norm_scale * gathered.reshape(width)
    return (back[0], back[1], d_filt, decay_grad, d_out_weight)


def solution(mesh):
    in_specs = (
        P("seq", "tp"),
        P("seq", "tp"),
        P("seq", "tp"),
        P(None, "tp"),
        P("seq", "tp"),
        P("tp"),
    )
    out_specs = (P("seq", "tp"), P("seq", "tp"), P("seq", "tp"), P("tp"), P("seq", "tp"))
    return jax.shard_map(
        on_device, mesh=mesh, in_specs=in_specs, out_specs=out_specs, check_vma=False
    )
```

```python
import math

import jax
import jax.numpy as jnp
from jax import lax
from jax.sharding import PartitionSpec as P

HIGHEST = lax.Precision.HIGHEST
TWO_PI = 2.0 * math.pi


def angles(left, right, modulus):
    index = left[:, None] * right[None, :] % modulus
    phase = index.astype(jnp.float32) * (TWO_PI / modulus)
    return jnp.cos(phase), jnp.sin(phase)


def to_channels(block, parts):
    lead = block.shape[:-2]
    tok_rows, width = block.shape[-2:]
    nd = len(lead)
    split = block.reshape(lead + (tok_rows, parts, width // parts))
    split = jnp.transpose(split, tuple(range(nd)) + (nd + 1, nd + 2, nd))
    return lax.all_to_all(split, "seq", split_axis=nd, concat_axis=nd, tiled=True)


def to_tokens(block, parts):
    lead = block.shape[:-3]
    _, sub, tok_rows = block.shape[-3:]
    nd = len(lead)
    moved = lax.all_to_all(block, "seq", split_axis=nd, concat_axis=nd, tiled=True)
    moved = moved.reshape(lead + (parts * sub, tok_rows))
    return jnp.transpose(moved, tuple(range(nd)) + (nd + 1, nd))


class Dft:
    def __init__(self, parts, rows):
        outer = 2 * parts
        self.n = outer * rows
        self.rows = rows
        p_idx = jnp.arange(parts, dtype=jnp.int32)
        k1_idx = jnp.arange(outer, dtype=jnp.int32)
        r_idx = jnp.arange(rows, dtype=jnp.int32)
        c1, s1 = angles(k1_idx, p_idx, outer)
        self.fwd_outer = jnp.concatenate([c1, -s1], axis=0)
        self.inv_outer = jnp.concatenate([c1.T, -s1.T], axis=1) / self.n
        self.twid_c, self.twid_s = angles(k1_idx, r_idx, self.n)
        gc, gs = angles(r_idx, r_idx, rows)
        self.fwd_inner = jnp.concatenate(
            [jnp.concatenate([gc, -gs], axis=1), jnp.concatenate([gs, gc], axis=1)], axis=0
        )
        self.inv_inner = jnp.concatenate(
            [jnp.concatenate([gc, gs], axis=1), jnp.concatenate([-gs, gc], axis=1)], axis=0
        )

    def forward(self, x):
        y = jnp.einsum("kp,fpcr->fkcr", self.fwd_outer, x, precision=HIGHEST)
        outer = self.fwd_outer.shape[0] // 2
        yr, yi = y[:, :outer], y[:, outer:]
        tc = self.twid_c[None, :, None, :]
        ts = self.twid_s[None, :, None, :]
        zr = yr * tc + yi * ts
        zi = yi * tc - yr * ts
        z = jnp.concatenate([zr, zi], axis=-1)
        out = jnp.einsum("fkcr,rq->fkcq", z, self.fwd_inner, precision=HIGHEST)
        return out[..., : self.rows], out[..., self.rows :]

    def inverse_real(self, zr, zi):
        z = jnp.concatenate([zr, zi], axis=-1)
        u = jnp.einsum("fkcq,qr->fkcr", z, self.inv_inner, precision=HIGHEST)
        ur, ui = u[..., : self.rows], u[..., self.rows :]
        tc = self.twid_c[None, :, None, :]
        ts = self.twid_s[None, :, None, :]
        vr = ur * tc - ui * ts
        vi = ur * ts + ui * tc
        v = jnp.concatenate([vr, vi], axis=1)
        return jnp.einsum("pk,fkcr->fpcr", self.inv_outer, v, precision=HIGHEST)


def on_device(values, gate, out_grad, out_weight, filt, decay):
    tok_rows, width = values.shape
    parts = lax.axis_size("seq")
    my_index = lax.axis_index("seq")
    sub = width // parts
    length = tok_rows * parts
    norm_scale = 1.0 / math.sqrt(length)

    early = to_channels(jnp.stack([values, gate]), parts)
    filt_c = to_channels(filt, parts)

    full_grad = lax.all_gather(out_grad, "tp", axis=1, tiled=True)
    grad_y = jnp.dot(full_grad, out_weight, preferred_element_type=jnp.float32).astype(jnp.bfloat16)

    values_c = early[0].astype(jnp.float32)
    gate_c = early[1].astype(jnp.float32)

    my_decay = lax.dynamic_slice_in_dim(decay, my_index * sub, sub)
    tok = (
        jnp.arange(parts, dtype=jnp.int32)[:, None, None] * tok_rows
        + jnp.arange(tok_rows, dtype=jnp.int32)[None, None, :]
    )
    position = tok.astype(jnp.float32) / length
    window = jnp.exp(-my_decay[None, :, None] * position)
    kernel = filt_c * window * norm_scale

    dft = Dft(parts, tok_rows)
    vk_r, vk_i = dft.forward(jnp.stack([values_c, kernel]))
    v_r, k_r = vk_r[0], vk_r[1]
    v_i, k_i = vk_i[0], vk_i[1]
    conv_out = dft.inverse_real((v_r * k_r - v_i * k_i)[None], (v_r * k_i + v_i * k_r)[None])[0]
    gated_out = (gate_c * conv_out).astype(jnp.bfloat16)
    gated_home = to_tokens(gated_out, parts)
    term = lax.dot_general(
        full_grad, gated_home, (((0,), (0,)), ((), ())), preferred_element_type=jnp.float32
    )
    features = term.shape[0]
    core = my_index % 2
    halves = (term * norm_scale).reshape(parts // 2, 2, features // parts, width)
    keep = lax.dynamic_index_in_dim(halves, core, axis=1, keepdims=False)
    send = lax.dynamic_index_in_dim(halves, 1 - core, axis=1, keepdims=False)
    pairs = [(i, i ^ 1) for i in range(parts)]
    pair_sum = keep + lax.ppermute(send, "seq", pairs)
    groups = [list(range(0, parts, 2)), list(range(1, parts, 2))]
    d_out_weight = lax.psum_scatter(
        pair_sum.reshape(features // 2, width), "seq", scatter_dimension=0, tiled=True,
        axis_index_groups=groups,
    )

    grad_c = to_channels(grad_y, parts).astype(jnp.float32)
    gated_grad = grad_c * gate_c
    g_r, g_i = dft.forward(gated_grad[None])
    g_r, g_i = g_r[0], g_i[0]
    prod_r = jnp.stack([k_r * g_r + k_i * g_i, v_r * g_r + v_i * g_i])
    prod_i = jnp.stack([k_r * g_i - k_i * g_r, v_r * g_i - v_i * g_r])
    conv = dft.inverse_real(prod_r, prod_i)
    conv_grad, kernel_grad = conv[0], conv[1]

    d_values = conv_grad.astype(jnp.bfloat16)
    d_gate = (grad_c * conv_out).astype(jnp.bfloat16)
    d_filt_c = kernel_grad * window * norm_scale
    decay_part = jnp.sum(position * kernel_grad * kernel, axis=(0, 2))

    back = to_tokens(jnp.stack([d_values, d_gate]), parts)
    d_filt = to_tokens(d_filt_c, parts)
    spread = jnp.broadcast_to(decay_part[None, :], (parts, sub))
    gathered = lax.all_to_all(spread, "seq", split_axis=0, concat_axis=0, tiled=True)
    decay_grad = -norm_scale * gathered.reshape(width)
    return (back[0], back[1], d_filt, decay_grad, d_out_weight)


def solution(mesh):
    in_specs = (
        P("seq", "tp"),
        P("seq", "tp"),
        P("seq", "tp"),
        P(None, "tp"),
        P("seq", "tp"),
        P("tp"),
    )
    out_specs = (P("seq", "tp"), P("seq", "tp"), P("seq", "tp"), P("tp"), P("seq", "tp"))
    return jax.shard_map(
        on_device, mesh=mesh, in_specs=in_specs, out_specs=out_specs, check_vma=False
    )
```

```python
import math

import jax
import jax.numpy as jnp
from jax import lax
from jax.sharding import PartitionSpec as P

HIGHEST = lax.Precision.HIGHEST
TWO_PI = 2.0 * math.pi


def angles(left, right, modulus):
    index = left[:, None] * right[None, :] % modulus
    phase = index.astype(jnp.float32) * (TWO_PI / modulus)
    return jnp.cos(phase), jnp.sin(phase)


def to_channels(block, parts):
    lead = block.shape[:-2]
    tok_rows, width = block.shape[-2:]
    nd = len(lead)
    split = block.reshape(lead + (tok_rows, parts, width // parts))
    split = jnp.transpose(split, tuple(range(nd)) + (nd + 1, nd + 2, nd))
    return lax.all_to_all(split, "seq", split_axis=nd, concat_axis=nd, tiled=True)


def to_tokens(block, parts):
    lead = block.shape[:-3]
    _, sub, tok_rows = block.shape[-3:]
    nd = len(lead)
    moved = lax.all_to_all(block, "seq", split_axis=nd, concat_axis=nd, tiled=True)
    moved = moved.reshape(lead + (parts * sub, tok_rows))
    return jnp.transpose(moved, tuple(range(nd)) + (nd + 1, nd))


class Dft:
    def __init__(self, parts, rows):
        outer = 2 * parts
        self.n = outer * rows
        self.rows = rows
        p_idx = jnp.arange(parts, dtype=jnp.int32)
        k1_idx = jnp.arange(outer, dtype=jnp.int32)
        r_idx = jnp.arange(rows, dtype=jnp.int32)
        c1, s1 = angles(k1_idx, p_idx, outer)
        self.fwd_outer = jnp.concatenate([c1, -s1], axis=0)
        self.inv_outer = jnp.concatenate([c1.T, -s1.T], axis=1) / self.n
        self.twid_c, self.twid_s = angles(k1_idx, r_idx, self.n)
        gc, gs = angles(r_idx, r_idx, rows)
        self.fwd_inner = jnp.concatenate(
            [jnp.concatenate([gc, -gs], axis=1), jnp.concatenate([gs, gc], axis=1)], axis=0
        )
        self.inv_inner = jnp.concatenate(
            [jnp.concatenate([gc, gs], axis=1), jnp.concatenate([-gs, gc], axis=1)], axis=0
        )

    def forward(self, x):
        y = jnp.einsum("kp,fpcr->fkcr", self.fwd_outer, x, precision=HIGHEST)
        outer = self.fwd_outer.shape[0] // 2
        yr, yi = y[:, :outer], y[:, outer:]
        tc = self.twid_c[None, :, None, :]
        ts = self.twid_s[None, :, None, :]
        zr = yr * tc + yi * ts
        zi = yi * tc - yr * ts
        z = jnp.concatenate([zr, zi], axis=-1)
        out = jnp.einsum("fkcr,rq->fkcq", z, self.fwd_inner, precision=HIGHEST)
        return out[..., : self.rows], out[..., self.rows :]

    def inverse_real(self, zr, zi):
        z = jnp.concatenate([zr, zi], axis=-1)
        u = jnp.einsum("fkcq,qr->fkcr", z, self.inv_inner, precision=HIGHEST)
        ur, ui = u[..., : self.rows], u[..., self.rows :]
        tc = self.twid_c[None, :, None, :]
        ts = self.twid_s[None, :, None, :]
        vr = ur * tc - ui * ts
        vi = ur * ts + ui * tc
        v = jnp.concatenate([vr, vi], axis=1)
        return jnp.einsum("pk,fkcr->fpcr", self.inv_outer, v, precision=HIGHEST)


def pair_reduce(full_grad, gated_home, my_index, parts, norm_scale):
    width = gated_home.shape[1]
    half = width // 2
    core = my_index % 2
    pairs = [(i, i ^ 1) for i in range(parts)]
    groups = [list(range(0, parts, 2)), list(range(1, parts, 2))]
    keep_cols = lax.dynamic_slice_in_dim(gated_home, core * half, half, axis=1)
    send_cols = lax.dynamic_slice_in_dim(gated_home, (1 - core) * half, half, axis=1)
    dims = (((0,), (0,)), ((), ()))
    keep = lax.dot_general(full_grad, keep_cols, dims, preferred_element_type=jnp.float32)
    send = lax.dot_general(full_grad, send_cols, dims, preferred_element_type=jnp.float32)
    pair_sum = (keep + lax.ppermute(send, "seq", pairs)) * norm_scale
    rows = lax.psum_scatter(pair_sum, "seq", scatter_dimension=0, tiled=True, axis_index_groups=groups)
    block = rows.shape[0] // 2
    own = lax.dynamic_slice_in_dim(rows, core * block, block, axis=0)
    given = lax.dynamic_slice_in_dim(rows, (1 - core) * block, block, axis=0)
    got = lax.ppermute(given, "seq", pairs)
    return jnp.where(core == 0, jnp.concatenate([own, got], axis=1), jnp.concatenate([got, own], axis=1))


def on_device(values, gate, out_grad, out_weight, filt, decay):
    tok_rows, width = values.shape
    parts = lax.axis_size("seq")
    my_index = lax.axis_index("seq")
    sub = width // parts
    length = tok_rows * parts
    norm_scale = 1.0 / math.sqrt(length)

    early = to_channels(jnp.stack([values, gate]), parts)
    filt_c = to_channels(filt, parts)

    full_grad = lax.all_gather(out_grad, "tp", axis=1, tiled=True)
    grad_y = jnp.dot(full_grad, out_weight, preferred_element_type=jnp.float32).astype(jnp.bfloat16)

    values_c = early[0].astype(jnp.float32)
    gate_c = early[1].astype(jnp.float32)

    my_decay = lax.dynamic_slice_in_dim(decay, my_index * sub, sub)
    tok = (
        jnp.arange(parts, dtype=jnp.int32)[:, None, None] * tok_rows
        + jnp.arange(tok_rows, dtype=jnp.int32)[None, None, :]
    )
    position = tok.astype(jnp.float32) / length
    window = jnp.exp(-my_decay[None, :, None] * position)
    kernel = filt_c * window * norm_scale

    dft = Dft(parts, tok_rows)
    vk_r, vk_i = dft.forward(jnp.stack([values_c, kernel]))
    v_r, k_r = vk_r[0], vk_r[1]
    v_i, k_i = vk_i[0], vk_i[1]
    conv_out = dft.inverse_real((v_r * k_r - v_i * k_i)[None], (v_r * k_i + v_i * k_r)[None])[0]
    gated_out = (gate_c * conv_out).astype(jnp.bfloat16)
    gated_home = to_tokens(gated_out, parts)
    d_out_weight = pair_reduce(full_grad, gated_home, my_index, parts, norm_scale)

    grad_c = to_channels(grad_y, parts).astype(jnp.float32)
    gated_grad = grad_c * gate_c
    g_r, g_i = dft.forward(gated_grad[None])
    g_r, g_i = g_r[0], g_i[0]
    prod_r = jnp.stack([k_r * g_r + k_i * g_i, v_r * g_r + v_i * g_i])
    prod_i = jnp.stack([k_r * g_i - k_i * g_r, v_r * g_i - v_i * g_r])
    conv = dft.inverse_real(prod_r, prod_i)
    conv_grad, kernel_grad = conv[0], conv[1]

    d_values = conv_grad.astype(jnp.bfloat16)
    d_gate = (grad_c * conv_out).astype(jnp.bfloat16)
    d_filt_c = kernel_grad * window * norm_scale
    decay_part = jnp.sum(position * kernel_grad * kernel, axis=(0, 2))

    back = to_tokens(jnp.stack([d_values, d_gate]), parts)
    d_filt = to_tokens(d_filt_c, parts)
    spread = jnp.broadcast_to(decay_part[None, :], (parts, sub))
    gathered = lax.all_to_all(spread, "seq", split_axis=0, concat_axis=0, tiled=True)
    decay_grad = -norm_scale * gathered.reshape(width)
    return (back[0], back[1], d_filt, decay_grad, d_out_weight)


def solution(mesh):
    in_specs = (
        P("seq", "tp"),
        P("seq", "tp"),
        P("seq", "tp"),
        P(None, "tp"),
        P("seq", "tp"),
        P("tp"),
    )
    out_specs = (P("seq", "tp"), P("seq", "tp"), P("seq", "tp"), P("tp"), P("seq", "tp"))
    return jax.shard_map(
        on_device, mesh=mesh, in_specs=in_specs, out_specs=out_specs, check_vma=False
    )
```

```python
import math

import jax
import jax.numpy as jnp
from jax import lax
from jax.sharding import PartitionSpec as P

HIGHEST = lax.Precision.HIGHEST
TWO_PI = 2.0 * math.pi


def angles(left, right, modulus):
    index = left[:, None] * right[None, :] % modulus
    phase = index.astype(jnp.float32) * (TWO_PI / modulus)
    return jnp.cos(phase), jnp.sin(phase)


def to_channels(block, parts):
    lead = block.shape[:-2]
    tok_rows, width = block.shape[-2:]
    nd = len(lead)
    split = block.reshape(lead + (tok_rows, parts, width // parts))
    split = jnp.transpose(split, tuple(range(nd)) + (nd + 1, nd + 2, nd))
    return lax.all_to_all(split, "seq", split_axis=nd, concat_axis=nd, tiled=True)


def to_tokens(block, parts):
    lead = block.shape[:-3]
    _, sub, tok_rows = block.shape[-3:]
    nd = len(lead)
    moved = lax.all_to_all(block, "seq", split_axis=nd, concat_axis=nd, tiled=True)
    moved = moved.reshape(lead + (parts * sub, tok_rows))
    return jnp.transpose(moved, tuple(range(nd)) + (nd + 1, nd))


class Dft:
    def __init__(self, parts, rows):
        outer = 2 * parts
        self.n = outer * rows
        self.rows = rows
        p_idx = jnp.arange(parts, dtype=jnp.int32)
        k1_idx = jnp.arange(outer, dtype=jnp.int32)
        r_idx = jnp.arange(rows, dtype=jnp.int32)
        c1, s1 = angles(k1_idx, p_idx, outer)
        self.fwd_outer = jnp.concatenate([c1, -s1], axis=0)
        self.inv_outer = jnp.concatenate([c1.T, -s1.T], axis=1) / self.n
        self.twid_c, self.twid_s = angles(k1_idx, r_idx, self.n)
        gc, gs = angles(r_idx, r_idx, rows)
        self.fwd_inner = jnp.concatenate(
            [jnp.concatenate([gc, -gs], axis=1), jnp.concatenate([gs, gc], axis=1)], axis=0
        )
        self.inv_inner = jnp.concatenate(
            [jnp.concatenate([gc, gs], axis=1), jnp.concatenate([-gs, gc], axis=1)], axis=0
        )

    def forward(self, x):
        y = jnp.einsum("kp,fpcr->fkcr", self.fwd_outer, x, precision=HIGHEST)
        outer = self.fwd_outer.shape[0] // 2
        yr, yi = y[:, :outer], y[:, outer:]
        tc = self.twid_c[None, :, None, :]
        ts = self.twid_s[None, :, None, :]
        zr = yr * tc + yi * ts
        zi = yi * tc - yr * ts
        z = jnp.concatenate([zr, zi], axis=-1)
        out = jnp.einsum("fkcr,rq->fkcq", z, self.fwd_inner, precision=HIGHEST)
        return out[..., : self.rows], out[..., self.rows :]

    def inverse_real(self, zr, zi):
        z = jnp.concatenate([zr, zi], axis=-1)
        u = jnp.einsum("fkcq,qr->fkcr", z, self.inv_inner, precision=HIGHEST)
        ur, ui = u[..., : self.rows], u[..., self.rows :]
        tc = self.twid_c[None, :, None, :]
        ts = self.twid_s[None, :, None, :]
        vr = ur * tc - ui * ts
        vi = ur * ts + ui * tc
        v = jnp.concatenate([vr, vi], axis=1)
        return jnp.einsum("pk,fkcr->fpcr", self.inv_outer, v, precision=HIGHEST)


def pair_products(full_grad, gated_home, core):
    half = gated_home.shape[1] // 2
    keep_cols = lax.dynamic_slice_in_dim(gated_home, core * half, half, axis=1)
    send_cols = lax.dynamic_slice_in_dim(gated_home, (1 - core) * half, half, axis=1)
    dims = (((0,), (0,)), ((), ()))
    keep = lax.dot_general(full_grad, keep_cols, dims, preferred_element_type=jnp.float32)
    send = lax.dot_general(full_grad, send_cols, dims, preferred_element_type=jnp.float32)
    return keep, send


def pair_reduce(keep, send, core, parts, norm_scale):
    pairs = [(i, i ^ 1) for i in range(parts)]
    groups = [list(range(0, parts, 2)), list(range(1, parts, 2))]
    pair_sum = (keep + lax.ppermute(send, "seq", pairs)) * norm_scale
    rows = lax.psum_scatter(pair_sum, "seq", scatter_dimension=0, tiled=True, axis_index_groups=groups)
    block = rows.shape[0] // 2
    own = lax.dynamic_slice_in_dim(rows, core * block, block, axis=0)
    given = lax.dynamic_slice_in_dim(rows, (1 - core) * block, block, axis=0)
    got = lax.ppermute(given, "seq", pairs)
    return jnp.where(core == 0, jnp.concatenate([own, got], axis=1), jnp.concatenate([got, own], axis=1))

def on_device(values, gate, out_grad, out_weight, filt, decay):
    tok_rows, width = values.shape
    parts = lax.axis_size("seq")
    my_index = lax.axis_index("seq")
    sub = width // parts
    length = tok_rows * parts
    norm_scale = 1.0 / math.sqrt(length)

    early = to_channels(
        jnp.stack([values.astype(jnp.float32), gate.astype(jnp.float32), filt]), parts
    )
    filt_c = early[2]

    full_grad = lax.all_gather(out_grad, "tp", axis=1, tiled=True)
    grad_y = jnp.dot(full_grad, out_weight, preferred_element_type=jnp.float32).astype(jnp.bfloat16)

    values_c = early[0]
    gate_c = early[1]

    my_decay = lax.dynamic_slice_in_dim(decay, my_index * sub, sub)
    tok = (
        jnp.arange(parts, dtype=jnp.int32)[:, None, None] * tok_rows
        + jnp.arange(tok_rows, dtype=jnp.int32)[None, None, :]
    )
    position = tok.astype(jnp.float32) / length
    window = jnp.exp(-my_decay[None, :, None] * position)
    kernel = filt_c * window * norm_scale

    dft = Dft(parts, tok_rows)
    vk_r, vk_i = dft.forward(jnp.stack([values_c, kernel]))
    v_r, k_r = vk_r[0], vk_r[1]
    v_i, k_i = vk_i[0], vk_i[1]
    conv_out = dft.inverse_real((v_r * k_r - v_i * k_i)[None], (v_r * k_i + v_i * k_r)[None])[0]
    gated_out = (gate_c * conv_out).astype(jnp.bfloat16)
    gated_home = to_tokens(gated_out, parts)
    core = my_index % 2
    keep, send, grad_y = lax.optimization_barrier(pair_products(full_grad, gated_home, core) + (grad_y,))
    d_out_weight = pair_reduce(keep, send, core, parts, norm_scale)

    grad_c = to_channels(grad_y, parts).astype(jnp.float32)
    gated_grad = grad_c * gate_c
    g_r, g_i = dft.forward(gated_grad[None])
    g_r, g_i = g_r[0], g_i[0]
    prod_r = jnp.stack([k_r * g_r + k_i * g_i, v_r * g_r + v_i * g_i])
    prod_i = jnp.stack([k_r * g_i - k_i * g_r, v_r * g_i - v_i * g_r])
    conv = dft.inverse_real(prod_r, prod_i)
    conv_grad, kernel_grad = conv[0], conv[1]

    d_values = conv_grad.astype(jnp.bfloat16)
    d_gate = (grad_c * conv_out).astype(jnp.bfloat16)
    d_filt_c = kernel_grad * window * norm_scale
    decay_part = jnp.sum(position * kernel_grad * kernel, axis=(0, 2))

    back = to_tokens(jnp.stack([d_values, d_gate]), parts)
    d_filt = to_tokens(d_filt_c, parts)
    spread = jnp.broadcast_to(decay_part[None, :], (parts, sub))
    gathered = lax.all_to_all(spread, "seq", split_axis=0, concat_axis=0, tiled=True)
    decay_grad = -norm_scale * gathered.reshape(width)
    return (back[0], back[1], d_filt, decay_grad, d_out_weight)


def solution(mesh):
    in_specs = (
        P("seq", "tp"),
        P("seq", "tp"),
        P("seq", "tp"),
        P(None, "tp"),
        P("seq", "tp"),
        P("tp"),
    )
    out_specs = (P("seq", "tp"), P("seq", "tp"), P("seq", "tp"), P("tp"), P("seq", "tp"))
    return jax.shard_map(
        on_device, mesh=mesh, in_specs=in_specs, out_specs=out_specs, check_vma=False
    )
```

```python
import math

import jax
import jax.numpy as jnp
from jax import lax
from jax.sharding import PartitionSpec as P

HIGHEST = lax.Precision.HIGHEST
TWO_PI = 2.0 * math.pi


def angles(left, right, modulus):
    index = left[:, None] * right[None, :] % modulus
    phase = index.astype(jnp.float32) * (TWO_PI / modulus)
    return jnp.cos(phase), jnp.sin(phase)


def split_blocks(block, parts):
    lead = block.shape[:-2]
    tok_rows, width = block.shape[-2:]
    nd = len(lead)
    split = block.reshape(lead + (tok_rows, parts, width // parts))
    return jnp.transpose(split, tuple(range(nd)) + (nd + 1, nd + 2, nd))


def to_channels(block, parts):
    nd = block.ndim - 2
    split = split_blocks(block, parts)
    return lax.all_to_all(split, "seq", split_axis=nd, concat_axis=nd, tiled=True)


def to_tokens(block, parts):
    lead = block.shape[:-3]
    _, sub, tok_rows = block.shape[-3:]
    nd = len(lead)
    moved = lax.all_to_all(block, "seq", split_axis=nd, concat_axis=nd, tiled=True)
    moved = moved.reshape(lead + (parts * sub, tok_rows))
    return jnp.transpose(moved, tuple(range(nd)) + (nd + 1, nd))


class Dft:
    def __init__(self, parts, rows):
        outer = 2 * parts
        self.n = outer * rows
        self.rows = rows
        p_idx = jnp.arange(parts, dtype=jnp.int32)
        k1_idx = jnp.arange(outer, dtype=jnp.int32)
        r_idx = jnp.arange(rows, dtype=jnp.int32)
        c1, s1 = angles(k1_idx, p_idx, outer)
        self.fwd_outer = jnp.concatenate([c1, -s1], axis=0)
        self.inv_outer = jnp.concatenate([c1.T, -s1.T], axis=1) / self.n
        self.twid_c, self.twid_s = angles(k1_idx, r_idx, self.n)
        gc, gs = angles(r_idx, r_idx, rows)
        self.fwd_inner = jnp.concatenate(
            [jnp.concatenate([gc, -gs], axis=1), jnp.concatenate([gs, gc], axis=1)], axis=0
        )
        self.inv_inner = jnp.concatenate(
            [jnp.concatenate([gc, gs], axis=1), jnp.concatenate([-gs, gc], axis=1)], axis=0
        )

    def forward(self, x):
        y = jnp.einsum("kp,fpcr->fkcr", self.fwd_outer, x, precision=HIGHEST)
        outer = self.fwd_outer.shape[0] // 2
        yr, yi = y[:, :outer], y[:, outer:]
        tc = self.twid_c[None, :, None, :]
        ts = self.twid_s[None, :, None, :]
        zr = yr * tc + yi * ts
        zi = yi * tc - yr * ts
        z = jnp.concatenate([zr, zi], axis=-1)
        out = jnp.einsum("fkcr,rq->fkcq", z, self.fwd_inner, precision=HIGHEST)
        return out[..., : self.rows], out[..., self.rows :]

    def inverse_real(self, zr, zi):
        z = jnp.concatenate([zr, zi], axis=-1)
        u = jnp.einsum("fkcq,qr->fkcr", z, self.inv_inner, precision=HIGHEST)
        ur, ui = u[..., : self.rows], u[..., self.rows :]
        tc = self.twid_c[None, :, None, :]
        ts = self.twid_s[None, :, None, :]
        vr = ur * tc - ui * ts
        vi = ur * ts + ui * tc
        v = jnp.concatenate([vr, vi], axis=1)
        return jnp.einsum("pk,fkcr->fpcr", self.inv_outer, v, precision=HIGHEST)


def pair_products(full_grad, gated_home, core):
    half = gated_home.shape[1] // 2
    keep_cols = lax.dynamic_slice_in_dim(gated_home, core * half, half, axis=1)
    send_cols = lax.dynamic_slice_in_dim(gated_home, (1 - core) * half, half, axis=1)
    dims = (((0,), (0,)), ((), ()))
    keep = lax.dot_general(full_grad, keep_cols, dims, preferred_element_type=jnp.float32)
    send = lax.dot_general(full_grad, send_cols, dims, preferred_element_type=jnp.float32)
    return keep, send


def pair_reduce(keep, send, core, parts, norm_scale):
    pairs = [(i, i ^ 1) for i in range(parts)]
    groups = [list(range(0, parts, 2)), list(range(1, parts, 2))]
    pair_sum = (keep + lax.ppermute(send, "seq", pairs)) * norm_scale
    rows = lax.psum_scatter(pair_sum, "seq", scatter_dimension=0, tiled=True, axis_index_groups=groups)
    block = rows.shape[0] // 2
    own = lax.dynamic_slice_in_dim(rows, core * block, block, axis=0)
    given = lax.dynamic_slice_in_dim(rows, (1 - core) * block, block, axis=0)
    got = lax.ppermute(given, "seq", pairs)
    return jnp.where(core == 0, jnp.concatenate([own, got], axis=1), jnp.concatenate([got, own], axis=1))

def on_device(values, gate, out_grad, out_weight, filt, decay):
    tok_rows, width = values.shape
    parts = lax.axis_size("seq")
    my_index = lax.axis_index("seq")
    sub = width // parts
    length = tok_rows * parts
    norm_scale = 1.0 / math.sqrt(length)

    early = to_channels(
        jnp.stack([values.astype(jnp.float32), gate.astype(jnp.float32), filt]), parts
    )
    filt_c = early[2]

    full_grad = lax.all_gather(out_grad, "tp", axis=1, tiled=True)
    grad_y = jnp.dot(full_grad, out_weight, preferred_element_type=jnp.float32).astype(jnp.bfloat16)

    values_c = early[0]
    gate_c = early[1]

    my_decay = lax.dynamic_slice_in_dim(decay, my_index * sub, sub)
    tok = (
        jnp.arange(parts, dtype=jnp.int32)[:, None, None] * tok_rows
        + jnp.arange(tok_rows, dtype=jnp.int32)[None, None, :]
    )
    position = tok.astype(jnp.float32) / length
    window = jnp.exp(-my_decay[None, :, None] * position)
    kernel = filt_c * window * norm_scale

    dft = Dft(parts, tok_rows)
    vk_r, vk_i = dft.forward(jnp.stack([values_c, kernel]))
    v_r, k_r = vk_r[0], vk_r[1]
    v_i, k_i = vk_i[0], vk_i[1]
    conv_out = dft.inverse_real((v_r * k_r - v_i * k_i)[None], (v_r * k_i + v_i * k_r)[None])[0]
    gated_out = (gate_c * conv_out).astype(jnp.bfloat16)
    crossed = lax.all_to_all(
        jnp.stack([gated_out, split_blocks(grad_y, parts)]), "seq", split_axis=1, concat_axis=1,
        tiled=True,
    )
    gated_home = jnp.transpose(crossed[0].reshape(width, tok_rows))
    grad_c = crossed[1].astype(jnp.float32)
    core = my_index % 2
    keep, send = pair_products(full_grad, gated_home, core)
    d_out_weight = pair_reduce(keep, send, core, parts, norm_scale)

    gated_grad = grad_c * gate_c
    g_r, g_i = dft.forward(gated_grad[None])
    g_r, g_i = g_r[0], g_i[0]
    prod_r = jnp.stack([k_r * g_r + k_i * g_i, v_r * g_r + v_i * g_i])
    prod_i = jnp.stack([k_r * g_i - k_i * g_r, v_r * g_i - v_i * g_r])
    conv = dft.inverse_real(prod_r, prod_i)
    conv_grad, kernel_grad = conv[0], conv[1]

    d_values = conv_grad.astype(jnp.bfloat16)
    d_gate = (grad_c * conv_out).astype(jnp.bfloat16)
    d_filt_c = kernel_grad * window * norm_scale
    decay_part = jnp.sum(position * kernel_grad * kernel, axis=(0, 2))

    back = to_tokens(jnp.stack([d_values, d_gate]), parts)
    d_filt = to_tokens(d_filt_c, parts)
    spread = jnp.broadcast_to(decay_part[None, :], (parts, sub))
    gathered = lax.all_to_all(spread, "seq", split_axis=0, concat_axis=0, tiled=True)
    decay_grad = -norm_scale * gathered.reshape(width)
    return (back[0], back[1], d_filt, decay_grad, d_out_weight)


def solution(mesh):
    in_specs = (
        P("seq", "tp"),
        P("seq", "tp"),
        P("seq", "tp"),
        P(None, "tp"),
        P("seq", "tp"),
        P("tp"),
    )
    out_specs = (P("seq", "tp"), P("seq", "tp"), P("seq", "tp"), P("tp"), P("seq", "tp"))
    return jax.shard_map(
        on_device, mesh=mesh, in_specs=in_specs, out_specs=out_specs, check_vma=False
    )
```

```python
import math

import jax
import jax.numpy as jnp
from jax import lax
from jax.sharding import PartitionSpec as P

HIGHEST = lax.Precision.HIGHEST
TWO_PI = 2.0 * math.pi


def angles(left, right, modulus):
    index = left[:, None] * right[None, :] % modulus
    phase = index.astype(jnp.float32) * (TWO_PI / modulus)
    return jnp.cos(phase), jnp.sin(phase)


def to_channels(block, parts):
    lead = block.shape[:-2]
    tok_rows, width = block.shape[-2:]
    nd = len(lead)
    split = block.reshape(lead + (tok_rows, parts, width // parts))
    split = jnp.transpose(split, tuple(range(nd)) + (nd + 1, nd + 2, nd))
    return lax.all_to_all(split, "seq", split_axis=nd, concat_axis=nd, tiled=True)


def to_tokens(block, parts):
    lead = block.shape[:-3]
    _, sub, tok_rows = block.shape[-3:]
    nd = len(lead)
    moved = lax.all_to_all(block, "seq", split_axis=nd, concat_axis=nd, tiled=True)
    moved = moved.reshape(lead + (parts * sub, tok_rows))
    return jnp.transpose(moved, tuple(range(nd)) + (nd + 1, nd))


class Dft:
    def __init__(self, parts, rows):
        outer = 2 * parts
        self.n = outer * rows
        self.rows = rows
        p_idx = jnp.arange(parts, dtype=jnp.int32)
        k1_idx = jnp.arange(outer, dtype=jnp.int32)
        r_idx = jnp.arange(rows, dtype=jnp.int32)
        c1, s1 = angles(k1_idx, p_idx, outer)
        self.fwd_outer = jnp.concatenate([c1, -s1], axis=0)
        self.inv_outer = jnp.concatenate([c1.T, -s1.T], axis=1) / self.n
        self.twid_c, self.twid_s = angles(k1_idx, r_idx, self.n)
        gc, gs = angles(r_idx, r_idx, rows)
        self.fwd_inner = jnp.concatenate(
            [jnp.concatenate([gc, -gs], axis=1), jnp.concatenate([gs, gc], axis=1)], axis=0
        )
        self.inv_inner = jnp.concatenate(
            [jnp.concatenate([gc, gs], axis=1), jnp.concatenate([-gs, gc], axis=1)], axis=0
        )

    def forward(self, x):
        y = jnp.einsum("kp,fpcr->fkcr", self.fwd_outer, x, precision=HIGHEST)
        outer = self.fwd_outer.shape[0] // 2
        yr, yi = y[:, :outer], y[:, outer:]
        tc = self.twid_c[None, :, None, :]
        ts = self.twid_s[None, :, None, :]
        zr = yr * tc + yi * ts
        zi = yi * tc - yr * ts
        z = jnp.concatenate([zr, zi], axis=-1)
        out = jnp.einsum("fkcr,rq->fkcq", z, self.fwd_inner, precision=HIGHEST)
        return out[..., : self.rows], out[..., self.rows :]

    def inverse_real(self, zr, zi):
        z = jnp.concatenate([zr, zi], axis=-1)
        u = jnp.einsum("fkcq,qr->fkcr", z, self.inv_inner, precision=HIGHEST)
        ur, ui = u[..., : self.rows], u[..., self.rows :]
        tc = self.twid_c[None, :, None, :]
        ts = self.twid_s[None, :, None, :]
        vr = ur * tc - ui * ts
        vi = ur * ts + ui * tc
        v = jnp.concatenate([vr, vi], axis=1)
        return jnp.einsum("pk,fkcr->fpcr", self.inv_outer, v, precision=HIGHEST)


def pair_products(full_grad, gated_home, core):
    half = gated_home.shape[1] // 2
    keep_cols = lax.dynamic_slice_in_dim(gated_home, core * half, half, axis=1)
    send_cols = lax.dynamic_slice_in_dim(gated_home, (1 - core) * half, half, axis=1)
    dims = (((0,), (0,)), ((), ()))
    keep = lax.dot_general(full_grad, keep_cols, dims, preferred_element_type=jnp.float32)
    send = lax.dot_general(full_grad, send_cols, dims, preferred_element_type=jnp.float32)
    return keep, send


def pair_reduce(keep, send, core, parts, norm_scale):
    pairs = [(i, i ^ 1) for i in range(parts)]
    groups = [list(range(0, parts, 2)), list(range(1, parts, 2))]
    pair_sum = (keep + lax.ppermute(send, "seq", pairs)) * norm_scale
    rows = lax.psum_scatter(pair_sum, "seq", scatter_dimension=0, tiled=True, axis_index_groups=groups)
    block = rows.shape[0] // 2
    own = lax.dynamic_slice_in_dim(rows, core * block, block, axis=0)
    given = lax.dynamic_slice_in_dim(rows, (1 - core) * block, block, axis=0)
    got = lax.ppermute(given, "seq", pairs)
    return jnp.where(core == 0, jnp.concatenate([own, got], axis=1), jnp.concatenate([got, own], axis=1))

def on_device(values, gate, out_grad, out_weight, filt, decay):
    tok_rows, width = values.shape
    parts = lax.axis_size("seq")
    my_index = lax.axis_index("seq")
    sub = width // parts
    length = tok_rows * parts
    norm_scale = 1.0 / math.sqrt(length)

    early = to_channels(jnp.stack([values.astype(jnp.float32), filt]), parts)
    filt_c = early[1]
    gate_c = to_channels(gate, parts).astype(jnp.float32)

    full_grad = lax.all_gather(out_grad, "tp", axis=1, tiled=True)
    grad_y = jnp.dot(full_grad, out_weight, preferred_element_type=jnp.float32).astype(jnp.bfloat16)

    values_c = early[0]

    my_decay = lax.dynamic_slice_in_dim(decay, my_index * sub, sub)
    tok = (
        jnp.arange(parts, dtype=jnp.int32)[:, None, None] * tok_rows
        + jnp.arange(tok_rows, dtype=jnp.int32)[None, None, :]
    )
    position = tok.astype(jnp.float32) / length
    window = jnp.exp(-my_decay[None, :, None] * position)
    kernel = filt_c * window * norm_scale

    dft = Dft(parts, tok_rows)
    vk_r, vk_i = dft.forward(jnp.stack([values_c, kernel]))
    v_r, k_r = vk_r[0], vk_r[1]
    v_i, k_i = vk_i[0], vk_i[1]
    conv_out = dft.inverse_real((v_r * k_r - v_i * k_i)[None], (v_r * k_i + v_i * k_r)[None])[0]
    gated_out = (gate_c * conv_out).astype(jnp.bfloat16)
    gated_home = to_tokens(gated_out, parts)
    core = my_index % 2
    keep, send, grad_y = lax.optimization_barrier(pair_products(full_grad, gated_home, core) + (grad_y,))
    d_out_weight = pair_reduce(keep, send, core, parts, norm_scale)

    grad_c = to_channels(grad_y, parts).astype(jnp.float32)
    gated_grad = grad_c * gate_c
    g_r, g_i = dft.forward(gated_grad[None])
    g_r, g_i = g_r[0], g_i[0]
    prod_r = jnp.stack([k_r * g_r + k_i * g_i, v_r * g_r + v_i * g_i])
    prod_i = jnp.stack([k_r * g_i - k_i * g_r, v_r * g_i - v_i * g_r])
    conv = dft.inverse_real(prod_r, prod_i)
    conv_grad, kernel_grad = conv[0], conv[1]

    d_values = conv_grad.astype(jnp.bfloat16)
    d_gate = (grad_c * conv_out).astype(jnp.bfloat16)
    d_filt_c = kernel_grad * window * norm_scale
    decay_part = jnp.sum(position * kernel_grad * kernel, axis=(0, 2))

    back = to_tokens(
        jnp.stack([d_values.astype(jnp.float32), d_gate.astype(jnp.float32), d_filt_c]), parts
    )
    d_filt = back[2]
    spread = jnp.broadcast_to(decay_part[None, :], (parts, sub))
    gathered = lax.all_to_all(spread, "seq", split_axis=0, concat_axis=0, tiled=True)
    decay_grad = -norm_scale * gathered.reshape(width)
    return (
        back[0].astype(jnp.bfloat16), back[1].astype(jnp.bfloat16), d_filt, decay_grad, d_out_weight
    )


def solution(mesh):
    in_specs = (
        P("seq", "tp"),
        P("seq", "tp"),
        P("seq", "tp"),
        P(None, "tp"),
        P("seq", "tp"),
        P("tp"),
    )
    out_specs = (P("seq", "tp"), P("seq", "tp"), P("seq", "tp"), P("tp"), P("seq", "tp"))
    return jax.shard_map(
        on_device, mesh=mesh, in_specs=in_specs, out_specs=out_specs, check_vma=False
    )
```

```python
import math

import jax
import jax.numpy as jnp
from jax import lax
from jax.sharding import PartitionSpec as P

DFT_PRECISION = lax.Precision.HIGH
TWO_PI = 2.0 * math.pi


def angles(left, right, modulus):
    index = left[:, None] * right[None, :] % modulus
    phase = index.astype(jnp.float32) * (TWO_PI / modulus)
    return jnp.cos(phase), jnp.sin(phase)


def to_channels(block, parts):
    lead = block.shape[:-2]
    tok_rows, width = block.shape[-2:]
    nd = len(lead)
    split = block.reshape(lead + (tok_rows, parts, width // parts))
    split = jnp.transpose(split, tuple(range(nd)) + (nd + 1, nd + 2, nd))
    return lax.all_to_all(split, "seq", split_axis=nd, concat_axis=nd, tiled=True)


def to_tokens(block, parts):
    lead = block.shape[:-3]
    _, sub, tok_rows = block.shape[-3:]
    nd = len(lead)
    moved = lax.all_to_all(block, "seq", split_axis=nd, concat_axis=nd, tiled=True)
    moved = moved.reshape(lead + (parts * sub, tok_rows))
    return jnp.transpose(moved, tuple(range(nd)) + (nd + 1, nd))


class Dft:
    def __init__(self, parts, rows):
        outer = 2 * parts
        self.n = outer * rows
        self.rows = rows
        p_idx = jnp.arange(parts, dtype=jnp.int32)
        k1_idx = jnp.arange(outer, dtype=jnp.int32)
        r_idx = jnp.arange(rows, dtype=jnp.int32)
        c1, s1 = angles(k1_idx, p_idx, outer)
        self.fwd_outer = jnp.concatenate([c1, -s1], axis=0)
        self.inv_outer = jnp.concatenate([c1.T, -s1.T], axis=1) / self.n
        self.twid_c, self.twid_s = angles(k1_idx, r_idx, self.n)
        gc, gs = angles(r_idx, r_idx, rows)
        self.fwd_inner = jnp.concatenate(
            [jnp.concatenate([gc, -gs], axis=1), jnp.concatenate([gs, gc], axis=1)], axis=0
        )
        self.inv_inner = jnp.concatenate(
            [jnp.concatenate([gc, gs], axis=1), jnp.concatenate([-gs, gc], axis=1)], axis=0
        )

    def forward(self, x):
        y = jnp.einsum("kp,fpcr->fkcr", self.fwd_outer, x, precision=DFT_PRECISION)
        outer = self.fwd_outer.shape[0] // 2
        yr, yi = y[:, :outer], y[:, outer:]
        tc = self.twid_c[None, :, None, :]
        ts = self.twid_s[None, :, None, :]
        zr = yr * tc + yi * ts
        zi = yi * tc - yr * ts
        z = jnp.concatenate([zr, zi], axis=-1)
        out = jnp.einsum("fkcr,rq->fkcq", z, self.fwd_inner, precision=DFT_PRECISION)
        return out[..., : self.rows], out[..., self.rows :]

    def inverse_real(self, zr, zi):
        z = jnp.concatenate([zr, zi], axis=-1)
        u = jnp.einsum("fkcq,qr->fkcr", z, self.inv_inner, precision=DFT_PRECISION)
        ur, ui = u[..., : self.rows], u[..., self.rows :]
        tc = self.twid_c[None, :, None, :]
        ts = self.twid_s[None, :, None, :]
        vr = ur * tc - ui * ts
        vi = ur * ts + ui * tc
        v = jnp.concatenate([vr, vi], axis=1)
        return jnp.einsum("pk,fkcr->fpcr", self.inv_outer, v, precision=DFT_PRECISION)


def pair_products(full_grad, gated_home, core):
    half = gated_home.shape[1] // 2
    keep_cols = lax.dynamic_slice_in_dim(gated_home, core * half, half, axis=1)
    send_cols = lax.dynamic_slice_in_dim(gated_home, (1 - core) * half, half, axis=1)
    dims = (((0,), (0,)), ((), ()))
    keep = lax.dot_general(full_grad, keep_cols, dims, preferred_element_type=jnp.float32)
    send = lax.dot_general(full_grad, send_cols, dims, preferred_element_type=jnp.float32)
    return keep, send


def pair_reduce(keep, send, core, parts, norm_scale):
    pairs = [(i, i ^ 1) for i in range(parts)]
    groups = [list(range(0, parts, 2)), list(range(1, parts, 2))]
    pair_sum = (keep + lax.ppermute(send, "seq", pairs)) * norm_scale
    rows = lax.psum_scatter(pair_sum, "seq", scatter_dimension=0, tiled=True, axis_index_groups=groups)
    block = rows.shape[0] // 2
    own = lax.dynamic_slice_in_dim(rows, core * block, block, axis=0)
    given = lax.dynamic_slice_in_dim(rows, (1 - core) * block, block, axis=0)
    got = lax.ppermute(given, "seq", pairs)
    return jnp.where(core == 0, jnp.concatenate([own, got], axis=1), jnp.concatenate([got, own], axis=1))

def on_device(values, gate, out_grad, out_weight, filt, decay):
    tok_rows, width = values.shape
    parts = lax.axis_size("seq")
    my_index = lax.axis_index("seq")
    sub = width // parts
    length = tok_rows * parts
    norm_scale = 1.0 / math.sqrt(length)

    early = to_channels(jnp.stack([values.astype(jnp.float32), filt]), parts)
    filt_c = early[1]
    gate_c = to_channels(gate, parts).astype(jnp.float32)

    full_grad = lax.all_gather(out_grad, "tp", axis=1, tiled=True)
    grad_y = jnp.dot(full_grad, out_weight, preferred_element_type=jnp.float32).astype(jnp.bfloat16)

    values_c = early[0]

    my_decay = lax.dynamic_slice_in_dim(decay, my_index * sub, sub)
    tok = (
        jnp.arange(parts, dtype=jnp.int32)[:, None, None] * tok_rows
        + jnp.arange(tok_rows, dtype=jnp.int32)[None, None, :]
    )
    position = tok.astype(jnp.float32) / length
    window = jnp.exp(-my_decay[None, :, None] * position)
    kernel = filt_c * window * norm_scale

    dft = Dft(parts, tok_rows)
    vk_r, vk_i = dft.forward(jnp.stack([values_c, kernel]))
    v_r, k_r = vk_r[0], vk_r[1]
    v_i, k_i = vk_i[0], vk_i[1]
    conv_out = dft.inverse_real((v_r * k_r - v_i * k_i)[None], (v_r * k_i + v_i * k_r)[None])[0]
    gated_out = (gate_c * conv_out).astype(jnp.bfloat16)
    gated_home = to_tokens(gated_out, parts)
    core = my_index % 2
    keep, send, grad_y = lax.optimization_barrier(pair_products(full_grad, gated_home, core) + (grad_y,))
    d_out_weight = pair_reduce(keep, send, core, parts, norm_scale)

    grad_c = to_channels(grad_y, parts).astype(jnp.float32)
    gated_grad = grad_c * gate_c
    g_r, g_i = dft.forward(gated_grad[None])
    g_r, g_i = g_r[0], g_i[0]
    prod_r = jnp.stack([k_r * g_r + k_i * g_i, v_r * g_r + v_i * g_i])
    prod_i = jnp.stack([k_r * g_i - k_i * g_r, v_r * g_i - v_i * g_r])
    conv = dft.inverse_real(prod_r, prod_i)
    conv_grad, kernel_grad = conv[0], conv[1]

    d_values = conv_grad.astype(jnp.bfloat16)
    d_gate = (grad_c * conv_out).astype(jnp.bfloat16)
    d_filt_c = kernel_grad * window * norm_scale
    decay_part = jnp.sum(position * kernel_grad * kernel, axis=(0, 2))

    back = to_tokens(
        jnp.stack([d_values.astype(jnp.float32), d_gate.astype(jnp.float32), d_filt_c]), parts
    )
    d_filt = back[2]
    spread = jnp.broadcast_to(decay_part[None, :], (parts, sub))
    gathered = lax.all_to_all(spread, "seq", split_axis=0, concat_axis=0, tiled=True)
    decay_grad = -norm_scale * gathered.reshape(width)
    return (
        back[0].astype(jnp.bfloat16), back[1].astype(jnp.bfloat16), d_filt, decay_grad, d_out_weight
    )


def solution(mesh):
    in_specs = (
        P("seq", "tp"),
        P("seq", "tp"),
        P("seq", "tp"),
        P(None, "tp"),
        P("seq", "tp"),
        P("tp"),
    )
    out_specs = (P("seq", "tp"), P("seq", "tp"), P("seq", "tp"), P("tp"), P("seq", "tp"))
    return jax.shard_map(
        on_device, mesh=mesh, in_specs=in_specs, out_specs=out_specs, check_vma=False
    )
```

```python
import math

import jax
import jax.numpy as jnp
from jax import lax
from jax.sharding import PartitionSpec as P

HIGHEST = lax.Precision.HIGHEST
TWO_PI = 2.0 * math.pi


def angles(left, right, modulus):
    index = left[:, None] * right[None, :] % modulus
    phase = index.astype(jnp.float32) * (TWO_PI / modulus)
    return jnp.cos(phase), jnp.sin(phase)


def to_channels(block, parts):
    lead = block.shape[:-2]
    tok_rows, width = block.shape[-2:]
    nd = len(lead)
    split = block.reshape(lead + (tok_rows, parts, width // parts))
    split = jnp.transpose(split, tuple(range(nd)) + (nd + 1, nd + 2, nd))
    return lax.all_to_all(split, "seq", split_axis=nd, concat_axis=nd, tiled=True)


def to_tokens(block, parts):
    lead = block.shape[:-3]
    _, sub, tok_rows = block.shape[-3:]
    nd = len(lead)
    moved = lax.all_to_all(block, "seq", split_axis=nd, concat_axis=nd, tiled=True)
    moved = moved.reshape(lead + (parts * sub, tok_rows))
    return jnp.transpose(moved, tuple(range(nd)) + (nd + 1, nd))


class Dft:
    def __init__(self, parts, rows):
        outer = 2 * parts
        self.n = outer * rows
        self.rows = rows
        p_idx = jnp.arange(parts, dtype=jnp.int32)
        k1_idx = jnp.arange(outer, dtype=jnp.int32)
        r_idx = jnp.arange(rows, dtype=jnp.int32)
        c1, s1 = angles(k1_idx, p_idx, outer)
        self.fwd_outer = jnp.concatenate([c1, -s1], axis=0)
        self.inv_outer = jnp.concatenate([c1.T, -s1.T], axis=1) / self.n
        self.twid_c, self.twid_s = angles(k1_idx, r_idx, self.n)
        gc, gs = angles(r_idx, r_idx, rows)
        self.fwd_inner = jnp.concatenate(
            [jnp.concatenate([gc, -gs], axis=1), jnp.concatenate([gs, gc], axis=1)], axis=0
        )
        self.inv_inner = jnp.concatenate(
            [jnp.concatenate([gc, gs], axis=1), jnp.concatenate([-gs, gc], axis=1)], axis=0
        )

    def forward(self, x):
        y = jnp.einsum("kp,fpcr->fkcr", self.fwd_outer, x, precision=HIGHEST)
        outer = self.fwd_outer.shape[0] // 2
        yr, yi = y[:, :outer], y[:, outer:]
        tc = self.twid_c[None, :, None, :]
        ts = self.twid_s[None, :, None, :]
        zr = yr * tc + yi * ts
        zi = yi * tc - yr * ts
        z = jnp.concatenate([zr, zi], axis=-1)
        out = jnp.einsum("fkcr,rq->fkcq", z, self.fwd_inner, precision=HIGHEST)
        return out[..., : self.rows], out[..., self.rows :]

    def inverse_real(self, zr, zi):
        z = jnp.concatenate([zr, zi], axis=-1)
        u = jnp.einsum("fkcq,qr->fkcr", z, self.inv_inner, precision=HIGHEST)
        ur, ui = u[..., : self.rows], u[..., self.rows :]
        tc = self.twid_c[None, :, None, :]
        ts = self.twid_s[None, :, None, :]
        vr = ur * tc - ui * ts
        vi = ur * ts + ui * tc
        v = jnp.concatenate([vr, vi], axis=1)
        return jnp.einsum("pk,fkcr->fpcr", self.inv_outer, v, precision=HIGHEST)


def pair_products(full_grad, gated_home, core):
    half = gated_home.shape[1] // 2
    keep_cols = lax.dynamic_slice_in_dim(gated_home, core * half, half, axis=1)
    send_cols = lax.dynamic_slice_in_dim(gated_home, (1 - core) * half, half, axis=1)
    dims = (((0,), (0,)), ((), ()))
    keep = lax.dot_general(full_grad, keep_cols, dims, preferred_element_type=jnp.float32)
    send = lax.dot_general(full_grad, send_cols, dims, preferred_element_type=jnp.float32)
    return keep, send


def pair_reduce(keep, send, core, parts, norm_scale):
    pairs = [(i, i ^ 1) for i in range(parts)]
    groups = [list(range(0, parts, 2)), list(range(1, parts, 2))]
    pair_sum = (keep + lax.ppermute(send, "seq", pairs)) * norm_scale
    rows = lax.psum_scatter(pair_sum, "seq", scatter_dimension=0, tiled=True, axis_index_groups=groups)
    block = rows.shape[0] // 2
    own = lax.dynamic_slice_in_dim(rows, core * block, block, axis=0)
    given = lax.dynamic_slice_in_dim(rows, (1 - core) * block, block, axis=0)
    got = lax.ppermute(given, "seq", pairs)
    return jnp.where(core == 0, jnp.concatenate([own, got], axis=1), jnp.concatenate([got, own], axis=1))

def on_device(values, gate, out_grad, out_weight, filt, decay):
    tok_rows, width = values.shape
    parts = lax.axis_size("seq")
    my_index = lax.axis_index("seq")
    sub = width // parts
    length = tok_rows * parts
    norm_scale = 1.0 / math.sqrt(length)

    early = to_channels(jnp.stack([values.astype(jnp.float32), filt]), parts)
    filt_c = early[1]
    gate_c = to_channels(gate, parts).astype(jnp.float32)

    full_grad = lax.all_gather(out_grad, "tp", axis=1, tiled=True)
    grad_y = jnp.dot(full_grad, out_weight, preferred_element_type=jnp.float32).astype(jnp.bfloat16)

    values_c = early[0]

    my_decay = lax.dynamic_slice_in_dim(decay, my_index * sub, sub)
    tok = (
        jnp.arange(parts, dtype=jnp.int32)[:, None, None] * tok_rows
        + jnp.arange(tok_rows, dtype=jnp.int32)[None, None, :]
    )
    position = tok.astype(jnp.float32) / length
    window = jnp.exp(-my_decay[None, :, None] * position)
    kernel = filt_c * window * norm_scale

    dft = Dft(parts, tok_rows)
    vk_r, vk_i = dft.forward(jnp.stack([values_c, kernel]))
    v_r, k_r = vk_r[0], vk_r[1]
    v_i, k_i = vk_i[0], vk_i[1]
    conv_out = dft.inverse_real((v_r * k_r - v_i * k_i)[None], (v_r * k_i + v_i * k_r)[None])[0]
    gated_out = (gate_c * conv_out).astype(jnp.bfloat16)
    gated_home = to_tokens(gated_out, parts)
    core = my_index % 2
    keep, send, grad_y = lax.optimization_barrier(pair_products(full_grad, gated_home, core) + (grad_y,))
    d_out_weight = pair_reduce(keep, send, core, parts, norm_scale)

    grad_c = to_channels(grad_y, parts).astype(jnp.float32)
    gated_grad = grad_c * gate_c
    g_r, g_i = dft.forward(gated_grad[None])
    g_r, g_i = g_r[0], g_i[0]
    prod_r = jnp.stack([k_r * g_r + k_i * g_i, v_r * g_r + v_i * g_i])
    prod_i = jnp.stack([k_r * g_i - k_i * g_r, v_r * g_i - v_i * g_r])
    conv = dft.inverse_real(prod_r, prod_i)
    conv_grad, kernel_grad = conv[0], conv[1]

    d_values = conv_grad.astype(jnp.bfloat16)
    d_gate = (grad_c * conv_out).astype(jnp.bfloat16)
    d_filt_c = kernel_grad * window * norm_scale
    decay_part = jnp.sum(position * kernel_grad * kernel, axis=(0, 2))

    back = to_tokens(jnp.stack([d_values, d_gate]), parts)
    d_filt = to_tokens(d_filt_c, parts)
    spread = jnp.broadcast_to(decay_part[None, :], (parts, sub))
    gathered = lax.all_to_all(spread, "seq", split_axis=0, concat_axis=0, tiled=True)
    decay_grad = -norm_scale * gathered.reshape(width)
    return (back[0], back[1], d_filt, decay_grad, d_out_weight)


def solution(mesh):
    in_specs = (
        P("seq", "tp"),
        P("seq", "tp"),
        P("seq", "tp"),
        P(None, "tp"),
        P("seq", "tp"),
        P("tp"),
    )
    out_specs = (P("seq", "tp"), P("seq", "tp"), P("seq", "tp"), P("tp"), P("seq", "tp"))
    return jax.shard_map(
        on_device, mesh=mesh, in_specs=in_specs, out_specs=out_specs, check_vma=False
    )
```

```python
import math

import jax
import jax.numpy as jnp
from jax import lax
from jax.sharding import PartitionSpec as P

HIGHEST = lax.Precision.HIGHEST
TWO_PI = 2.0 * math.pi


def angles(left, right, modulus):
    index = left[:, None] * right[None, :] % modulus
    phase = index.astype(jnp.float32) * (TWO_PI / modulus)
    return jnp.cos(phase), jnp.sin(phase)


def to_channels(block, parts):
    lead = block.shape[:-2]
    tok_rows, width = block.shape[-2:]
    nd = len(lead)
    split = block.reshape(lead + (tok_rows, parts, width // parts))
    split = jnp.transpose(split, tuple(range(nd)) + (nd + 1, nd + 2, nd))
    return lax.all_to_all(split, "seq", split_axis=nd, concat_axis=nd, tiled=True)


def to_tokens(block, parts):
    lead = block.shape[:-3]
    _, sub, tok_rows = block.shape[-3:]
    nd = len(lead)
    moved = lax.all_to_all(block, "seq", split_axis=nd, concat_axis=nd, tiled=True)
    moved = moved.reshape(lead + (parts * sub, tok_rows))
    return jnp.transpose(moved, tuple(range(nd)) + (nd + 1, nd))


class Dft:
    def __init__(self, parts, rows):
        outer = 2 * parts
        self.n = outer * rows
        self.rows = rows
        p_idx = jnp.arange(parts, dtype=jnp.int32)
        k1_idx = jnp.arange(outer, dtype=jnp.int32)
        r_idx = jnp.arange(rows, dtype=jnp.int32)
        c1, s1 = angles(k1_idx, p_idx, outer)
        self.fwd_outer = jnp.concatenate([c1, -s1], axis=0)
        self.inv_outer = jnp.concatenate([c1.T, -s1.T], axis=1) / self.n
        self.twid_c, self.twid_s = angles(k1_idx, r_idx, self.n)
        gc, gs = angles(r_idx, r_idx, rows)
        self.fwd_inner = jnp.concatenate(
            [jnp.concatenate([gc, -gs], axis=1), jnp.concatenate([gs, gc], axis=1)], axis=0
        )
        self.inv_inner = jnp.concatenate(
            [jnp.concatenate([gc, gs], axis=1), jnp.concatenate([-gs, gc], axis=1)], axis=0
        )

    def forward(self, x):
        y = jnp.einsum("kp,fpcr->fkcr", self.fwd_outer, x, precision=HIGHEST)
        outer = self.fwd_outer.shape[0] // 2
        yr, yi = y[:, :outer], y[:, outer:]
        tc = self.twid_c[None, :, None, :]
        ts = self.twid_s[None, :, None, :]
        zr = yr * tc + yi * ts
        zi = yi * tc - yr * ts
        z = jnp.concatenate([zr, zi], axis=-1)
        out = jnp.einsum("fkcr,rq->fkcq", z, self.fwd_inner, precision=HIGHEST)
        return out[..., : self.rows], out[..., self.rows :]

    def inverse_real(self, zr, zi):
        z = jnp.concatenate([zr, zi], axis=-1)
        u = jnp.einsum("fkcq,qr->fkcr", z, self.inv_inner, precision=HIGHEST)
        ur, ui = u[..., : self.rows], u[..., self.rows :]
        tc = self.twid_c[None, :, None, :]
        ts = self.twid_s[None, :, None, :]
        vr = ur * tc - ui * ts
        vi = ur * ts + ui * tc
        v = jnp.concatenate([vr, vi], axis=1)
        return jnp.einsum("pk,fkcr->fpcr", self.inv_outer, v, precision=HIGHEST)


def pair_products(full_grad, gated_home, core):
    half = gated_home.shape[1] // 2
    keep_cols = lax.dynamic_slice_in_dim(gated_home, core * half, half, axis=1)
    send_cols = lax.dynamic_slice_in_dim(gated_home, (1 - core) * half, half, axis=1)
    dims = (((0,), (0,)), ((), ()))
    keep = lax.dot_general(full_grad, keep_cols, dims, preferred_element_type=jnp.float32)
    send = lax.dot_general(full_grad, send_cols, dims, preferred_element_type=jnp.float32)
    return keep, send


def pair_reduce(keep, send, core, parts, norm_scale):
    pairs = [(i, i ^ 1) for i in range(parts)]
    groups = [list(range(0, parts, 2)), list(range(1, parts, 2))]
    pair_sum = (keep + lax.ppermute(send, "seq", pairs)) * norm_scale
    rows = lax.psum_scatter(pair_sum, "seq", scatter_dimension=0, tiled=True, axis_index_groups=groups)
    block = rows.shape[0] // 2
    own = lax.dynamic_slice_in_dim(rows, core * block, block, axis=0)
    given = lax.dynamic_slice_in_dim(rows, (1 - core) * block, block, axis=0)
    got = lax.ppermute(given, "seq", pairs)
    return jnp.where(core == 0, jnp.concatenate([own, got], axis=1), jnp.concatenate([got, own], axis=1))

def on_device(values, gate, out_grad, out_weight, filt, decay):
    tok_rows, width = values.shape
    parts = lax.axis_size("seq")
    my_index = lax.axis_index("seq")
    sub = width // parts
    length = tok_rows * parts
    norm_scale = 1.0 / math.sqrt(length)

    early = to_channels(jnp.stack([values.astype(jnp.float32), filt]), parts)
    filt_c = early[1]
    gate_c = to_channels(gate, parts).astype(jnp.float32)

    full_grad = lax.all_gather(out_grad, "tp", axis=1, tiled=True)
    grad_y = jnp.dot(full_grad, out_weight, preferred_element_type=jnp.float32).astype(jnp.bfloat16)

    values_c = early[0]

    my_decay = lax.dynamic_slice_in_dim(decay, my_index * sub, sub)
    tok = (
        jnp.arange(parts, dtype=jnp.int32)[:, None, None] * tok_rows
        + jnp.arange(tok_rows, dtype=jnp.int32)[None, None, :]
    )
    position = tok.astype(jnp.float32) / length
    window = jnp.exp(-my_decay[None, :, None] * position)
    kernel = filt_c * window * norm_scale

    dft = Dft(parts, tok_rows)
    vk_r, vk_i = dft.forward(jnp.stack([values_c, kernel]))
    v_r, k_r = vk_r[0], vk_r[1]
    v_i, k_i = vk_i[0], vk_i[1]
    conv_out = dft.inverse_real((v_r * k_r - v_i * k_i)[None], (v_r * k_i + v_i * k_r)[None])[0]
    gated_out = (gate_c * conv_out).astype(jnp.bfloat16)
    gated_home = to_tokens(gated_out, parts)
    core = my_index % 2
    keep, send, grad_y = lax.optimization_barrier(pair_products(full_grad, gated_home, core) + (grad_y,))
    d_out_weight = pair_reduce(keep, send, core, parts, norm_scale)

    grad_c = to_channels(grad_y, parts).astype(jnp.float32)
    gated_grad = grad_c * gate_c
    g_r, g_i = dft.forward(gated_grad[None])
    g_r, g_i = g_r[0], g_i[0]
    prod_r = jnp.stack([k_r * g_r + k_i * g_i, v_r * g_r + v_i * g_i])
    prod_i = jnp.stack([k_r * g_i - k_i * g_r, v_r * g_i - v_i * g_r])
    conv = dft.inverse_real(prod_r, prod_i)
    conv_grad, kernel_grad = conv[0], conv[1]

    d_values = conv_grad.astype(jnp.bfloat16)
    d_gate = (grad_c * conv_out).astype(jnp.bfloat16)
    d_filt_c = kernel_grad * window * norm_scale
    decay_part = jnp.sum(position * kernel_grad * kernel, axis=(0, 2))

    back = to_tokens(jnp.stack([d_values, d_gate]), parts)
    lanes = 128
    slab = jnp.zeros((parts, sub, lanes), jnp.float32).at[:, :, 0].set(
        jnp.broadcast_to(decay_part[None, :], (parts, sub))
    )
    moved = lax.all_to_all(
        jnp.concatenate([d_filt_c, slab], axis=2), "seq", split_axis=0, concat_axis=0, tiled=True
    )
    d_filt = jnp.transpose(moved[:, :, :tok_rows].reshape(width, tok_rows))
    decay_grad = -norm_scale * moved[:, :, tok_rows].reshape(width)
    return (back[0], back[1], d_filt, decay_grad, d_out_weight)


def solution(mesh):
    in_specs = (
        P("seq", "tp"),
        P("seq", "tp"),
        P("seq", "tp"),
        P(None, "tp"),
        P("seq", "tp"),
        P("tp"),
    )
    out_specs = (P("seq", "tp"), P("seq", "tp"), P("seq", "tp"), P("tp"), P("seq", "tp"))
    return jax.shard_map(
        on_device, mesh=mesh, in_specs=in_specs, out_specs=out_specs, check_vma=False
    )
```

```python
import math

import jax
import jax.numpy as jnp
from jax import lax
from jax.sharding import PartitionSpec as P

HIGHEST = lax.Precision.HIGHEST
TWO_PI = 2.0 * math.pi


def angles(left, right, modulus):
    index = left[:, None] * right[None, :] % modulus
    phase = index.astype(jnp.float32) * (TWO_PI / modulus)
    return jnp.cos(phase), jnp.sin(phase)


def to_channels(block, parts):
    lead = block.shape[:-2]
    tok_rows, width = block.shape[-2:]
    nd = len(lead)
    split = block.reshape(lead + (tok_rows, parts, width // parts))
    split = jnp.transpose(split, tuple(range(nd)) + (nd + 1, nd + 2, nd))
    return lax.all_to_all(split, "seq", split_axis=nd, concat_axis=nd, tiled=True)


def to_tokens(block, parts):
    lead = block.shape[:-3]
    _, sub, tok_rows = block.shape[-3:]
    nd = len(lead)
    moved = lax.all_to_all(block, "seq", split_axis=nd, concat_axis=nd, tiled=True)
    moved = moved.reshape(lead + (parts * sub, tok_rows))
    return jnp.transpose(moved, tuple(range(nd)) + (nd + 1, nd))


class Dft:
    def __init__(self, parts, rows):
        outer = 2 * parts
        self.n = outer * rows
        self.rows = rows
        p_idx = jnp.arange(parts, dtype=jnp.int32)
        k1_idx = jnp.arange(outer, dtype=jnp.int32)
        r_idx = jnp.arange(rows, dtype=jnp.int32)
        c1, s1 = angles(k1_idx, p_idx, outer)
        self.fwd_outer = jnp.concatenate([c1, -s1], axis=0)
        self.inv_outer = jnp.concatenate([c1.T, -s1.T], axis=1) / self.n
        self.twid_c, self.twid_s = angles(k1_idx, r_idx, self.n)
        gc, gs = angles(r_idx, r_idx, rows)
        self.fwd_inner = jnp.concatenate(
            [jnp.concatenate([gc, -gs], axis=1), jnp.concatenate([gs, gc], axis=1)], axis=0
        )
        self.inv_inner = jnp.concatenate(
            [jnp.concatenate([gc, gs], axis=1), jnp.concatenate([-gs, gc], axis=1)], axis=0
        )

    def forward(self, x):
        y = jnp.einsum("kp,fpcr->fkcr", self.fwd_outer, x, precision=HIGHEST)
        outer = self.fwd_outer.shape[0] // 2
        yr, yi = y[:, :outer], y[:, outer:]
        tc = self.twid_c[None, :, None, :]
        ts = self.twid_s[None, :, None, :]
        zr = yr * tc + yi * ts
        zi = yi * tc - yr * ts
        z = jnp.concatenate([zr, zi], axis=-1)
        out = jnp.einsum("fkcr,rq->fkcq", z, self.fwd_inner, precision=HIGHEST)
        return out[..., : self.rows], out[..., self.rows :]

    def inverse_real(self, zr, zi):
        z = jnp.concatenate([zr, zi], axis=-1)
        u = jnp.einsum("fkcq,qr->fkcr", z, self.inv_inner, precision=HIGHEST)
        ur, ui = u[..., : self.rows], u[..., self.rows :]
        tc = self.twid_c[None, :, None, :]
        ts = self.twid_s[None, :, None, :]
        vr = ur * tc - ui * ts
        vi = ur * ts + ui * tc
        v = jnp.concatenate([vr, vi], axis=1)
        return jnp.einsum("pk,fkcr->fpcr", self.inv_outer, v, precision=HIGHEST)


def pair_products(full_grad, gated_home, core):
    half = gated_home.shape[1] // 2
    keep_cols = lax.dynamic_slice_in_dim(gated_home, core * half, half, axis=1)
    send_cols = lax.dynamic_slice_in_dim(gated_home, (1 - core) * half, half, axis=1)
    dims = (((0,), (0,)), ((), ()))
    keep = lax.dot_general(full_grad, keep_cols, dims, preferred_element_type=jnp.float32)
    send = lax.dot_general(full_grad, send_cols, dims, preferred_element_type=jnp.float32)
    return keep, send


def pair_reduce(keep, send, core, parts, norm_scale):
    pairs = [(i, i ^ 1) for i in range(parts)]
    groups = [list(range(0, parts, 2)), list(range(1, parts, 2))]
    sent = lax.ppermute((send * norm_scale).astype(jnp.bfloat16), "seq", pairs)
    pair_sum = keep * norm_scale + sent.astype(jnp.float32)
    rows = lax.psum_scatter(pair_sum, "seq", scatter_dimension=0, tiled=True, axis_index_groups=groups)
    block = rows.shape[0] // 2
    own = lax.dynamic_slice_in_dim(rows, core * block, block, axis=0)
    given = lax.dynamic_slice_in_dim(rows, (1 - core) * block, block, axis=0)
    got = lax.ppermute(given, "seq", pairs)
    return jnp.where(core == 0, jnp.concatenate([own, got], axis=1), jnp.concatenate([got, own], axis=1))

def on_device(values, gate, out_grad, out_weight, filt, decay):
    tok_rows, width = values.shape
    parts = lax.axis_size("seq")
    my_index = lax.axis_index("seq")
    sub = width // parts
    length = tok_rows * parts
    norm_scale = 1.0 / math.sqrt(length)

    early = to_channels(jnp.stack([values.astype(jnp.float32), filt]), parts)
    filt_c = early[1]
    gate_c = to_channels(gate, parts).astype(jnp.float32)

    full_grad = lax.all_gather(out_grad, "tp", axis=1, tiled=True)
    grad_y = jnp.dot(full_grad, out_weight, preferred_element_type=jnp.float32).astype(jnp.bfloat16)

    values_c = early[0]

    my_decay = lax.dynamic_slice_in_dim(decay, my_index * sub, sub)
    tok = (
        jnp.arange(parts, dtype=jnp.int32)[:, None, None] * tok_rows
        + jnp.arange(tok_rows, dtype=jnp.int32)[None, None, :]
    )
    position = tok.astype(jnp.float32) / length
    window = jnp.exp(-my_decay[None, :, None] * position)
    kernel = filt_c * window * norm_scale

    dft = Dft(parts, tok_rows)
    vk_r, vk_i = dft.forward(jnp.stack([values_c, kernel]))
    v_r, k_r = vk_r[0], vk_r[1]
    v_i, k_i = vk_i[0], vk_i[1]
    conv_out = dft.inverse_real((v_r * k_r - v_i * k_i)[None], (v_r * k_i + v_i * k_r)[None])[0]
    gated_out = (gate_c * conv_out).astype(jnp.bfloat16)
    gated_home = to_tokens(gated_out, parts)
    core = my_index % 2
    keep, send, grad_y = lax.optimization_barrier(pair_products(full_grad, gated_home, core) + (grad_y,))
    d_out_weight = pair_reduce(keep, send, core, parts, norm_scale)

    grad_c = to_channels(grad_y, parts).astype(jnp.float32)
    gated_grad = grad_c * gate_c
    g_r, g_i = dft.forward(gated_grad[None])
    g_r, g_i = g_r[0], g_i[0]
    prod_r = jnp.stack([k_r * g_r + k_i * g_i, v_r * g_r + v_i * g_i])
    prod_i = jnp.stack([k_r * g_i - k_i * g_r, v_r * g_i - v_i * g_r])
    conv = dft.inverse_real(prod_r, prod_i)
    conv_grad, kernel_grad = conv[0], conv[1]

    d_values = conv_grad.astype(jnp.bfloat16)
    d_gate = (grad_c * conv_out).astype(jnp.bfloat16)
    d_filt_c = kernel_grad * window * norm_scale
    decay_part = jnp.sum(position * kernel_grad * kernel, axis=(0, 2))

    back = to_tokens(jnp.stack([d_values, d_gate]), parts)
    lanes = 128
    slab = jnp.zeros((parts, sub, lanes), jnp.float32).at[:, :, 0].set(
        jnp.broadcast_to(decay_part[None, :], (parts, sub))
    )
    moved = lax.all_to_all(
        jnp.concatenate([d_filt_c, slab], axis=2), "seq", split_axis=0, concat_axis=0, tiled=True
    )
    d_filt = jnp.transpose(moved[:, :, :tok_rows].reshape(width, tok_rows))
    decay_grad = -norm_scale * moved[:, :, tok_rows].reshape(width)
    return (back[0], back[1], d_filt, decay_grad, d_out_weight)


def solution(mesh):
    in_specs = (
        P("seq", "tp"),
        P("seq", "tp"),
        P("seq", "tp"),
        P(None, "tp"),
        P("seq", "tp"),
        P("tp"),
    )
    out_specs = (P("seq", "tp"), P("seq", "tp"), P("seq", "tp"), P("tp"), P("seq", "tp"))
    return jax.shard_map(
        on_device, mesh=mesh, in_specs=in_specs, out_specs=out_specs, check_vma=False
    )
```

```python
import math

import jax
import jax.numpy as jnp
from jax import lax
from jax.sharding import PartitionSpec as P

HIGHEST = lax.Precision.HIGHEST
TWO_PI = 2.0 * math.pi


def angles(left, right, modulus):
    index = left[:, None] * right[None, :] % modulus
    phase = index.astype(jnp.float32) * (TWO_PI / modulus)
    return jnp.cos(phase), jnp.sin(phase)


def to_channels(block, parts):
    lead = block.shape[:-2]
    tok_rows, width = block.shape[-2:]
    nd = len(lead)
    split = block.reshape(lead + (tok_rows, parts, width // parts))
    split = jnp.transpose(split, tuple(range(nd)) + (nd + 1, nd + 2, nd))
    return lax.all_to_all(split, "seq", split_axis=nd, concat_axis=nd, tiled=True)


def to_tokens(block, parts):
    lead = block.shape[:-3]
    _, sub, tok_rows = block.shape[-3:]
    nd = len(lead)
    moved = lax.all_to_all(block, "seq", split_axis=nd, concat_axis=nd, tiled=True)
    moved = moved.reshape(lead + (parts * sub, tok_rows))
    return jnp.transpose(moved, tuple(range(nd)) + (nd + 1, nd))


class Dft:
    def __init__(self, parts, rows):
        outer = 2 * parts
        self.n = outer * rows
        self.rows = rows
        p_idx = jnp.arange(parts, dtype=jnp.int32)
        k1_idx = jnp.arange(outer, dtype=jnp.int32)
        r_idx = jnp.arange(rows, dtype=jnp.int32)
        c1, s1 = angles(k1_idx, p_idx, outer)
        self.fwd_outer = jnp.concatenate([c1, -s1], axis=0)
        self.inv_outer = jnp.concatenate([c1.T, -s1.T], axis=1) / self.n
        self.twid_c, self.twid_s = angles(k1_idx, r_idx, self.n)
        gc, gs = angles(r_idx, r_idx, rows)
        self.fwd_inner = jnp.concatenate(
            [jnp.concatenate([gc, -gs], axis=1), jnp.concatenate([gs, gc], axis=1)], axis=0
        )
        self.inv_inner = jnp.concatenate(
            [jnp.concatenate([gc, gs], axis=1), jnp.concatenate([-gs, gc], axis=1)], axis=0
        )

    def forward(self, x, precision=HIGHEST):
        y = jnp.einsum("kp,fpcr->fkcr", self.fwd_outer, x, precision=precision)
        outer = self.fwd_outer.shape[0] // 2
        yr, yi = y[:, :outer], y[:, outer:]
        tc = self.twid_c[None, :, None, :]
        ts = self.twid_s[None, :, None, :]
        zr = yr * tc + yi * ts
        zi = yi * tc - yr * ts
        z = jnp.concatenate([zr, zi], axis=-1)
        out = jnp.einsum("fkcr,rq->fkcq", z, self.fwd_inner, precision=precision)
        return out[..., : self.rows], out[..., self.rows :]

    def inverse_real(self, zr, zi, precision=HIGHEST):
        z = jnp.concatenate([zr, zi], axis=-1)
        u = jnp.einsum("fkcq,qr->fkcr", z, self.inv_inner, precision=precision)
        ur, ui = u[..., : self.rows], u[..., self.rows :]
        tc = self.twid_c[None, :, None, :]
        ts = self.twid_s[None, :, None, :]
        vr = ur * tc - ui * ts
        vi = ur * ts + ui * tc
        v = jnp.concatenate([vr, vi], axis=1)
        return jnp.einsum("pk,fkcr->fpcr", self.inv_outer, v, precision=precision)


def pair_products(full_grad, gated_home, core):
    half = gated_home.shape[1] // 2
    keep_cols = lax.dynamic_slice_in_dim(gated_home, core * half, half, axis=1)
    send_cols = lax.dynamic_slice_in_dim(gated_home, (1 - core) * half, half, axis=1)
    dims = (((0,), (0,)), ((), ()))
    keep = lax.dot_general(full_grad, keep_cols, dims, preferred_element_type=jnp.float32)
    send = lax.dot_general(full_grad, send_cols, dims, preferred_element_type=jnp.float32)
    return keep, send


def pair_reduce(keep, send, core, parts, norm_scale):
    pairs = [(i, i ^ 1) for i in range(parts)]
    groups = [list(range(0, parts, 2)), list(range(1, parts, 2))]
    sent = lax.ppermute((send * norm_scale).astype(jnp.bfloat16), "seq", pairs)
    pair_sum = keep * norm_scale + sent.astype(jnp.float32)
    rows = lax.psum_scatter(pair_sum, "seq", scatter_dimension=0, tiled=True, axis_index_groups=groups)
    block = rows.shape[0] // 2
    own = lax.dynamic_slice_in_dim(rows, core * block, block, axis=0)
    given = lax.dynamic_slice_in_dim(rows, (1 - core) * block, block, axis=0)
    got = lax.ppermute(given, "seq", pairs)
    return jnp.where(core == 0, jnp.concatenate([own, got], axis=1), jnp.concatenate([got, own], axis=1))

def on_device(values, gate, out_grad, out_weight, filt, decay):
    tok_rows, width = values.shape
    parts = lax.axis_size("seq")
    my_index = lax.axis_index("seq")
    sub = width // parts
    length = tok_rows * parts
    norm_scale = 1.0 / math.sqrt(length)

    early = to_channels(jnp.stack([values.astype(jnp.float32), filt]), parts)
    filt_c = early[1]
    gate_c = to_channels(gate, parts).astype(jnp.float32)

    full_grad = lax.all_gather(out_grad, "tp", axis=1, tiled=True)
    grad_y = jnp.dot(full_grad, out_weight, preferred_element_type=jnp.float32).astype(jnp.bfloat16)

    values_c = early[0]

    my_decay = lax.dynamic_slice_in_dim(decay, my_index * sub, sub)
    tok = (
        jnp.arange(parts, dtype=jnp.int32)[:, None, None] * tok_rows
        + jnp.arange(tok_rows, dtype=jnp.int32)[None, None, :]
    )
    position = tok.astype(jnp.float32) / length
    window = jnp.exp(-my_decay[None, :, None] * position)
    kernel = filt_c * window * norm_scale

    dft = Dft(parts, tok_rows)
    vk_r, vk_i = dft.forward(jnp.stack([values_c, kernel]))
    v_r, k_r = vk_r[0], vk_r[1]
    v_i, k_i = vk_i[0], vk_i[1]
    conv_out = dft.inverse_real((v_r * k_r - v_i * k_i)[None], (v_r * k_i + v_i * k_r)[None])[0]
    gated_out = (gate_c * conv_out).astype(jnp.bfloat16)
    gated_home = to_tokens(gated_out, parts)
    core = my_index % 2
    keep, send, grad_y = lax.optimization_barrier(pair_products(full_grad, gated_home, core) + (grad_y,))
    d_out_weight = pair_reduce(keep, send, core, parts, norm_scale)

    grad_c = to_channels(grad_y, parts).astype(jnp.float32)
    gated_grad = grad_c * gate_c
    g_r, g_i = dft.forward(gated_grad[None], lax.Precision.HIGH)
    g_r, g_i = g_r[0], g_i[0]
    prod_r = jnp.stack([k_r * g_r + k_i * g_i, v_r * g_r + v_i * g_i])
    prod_i = jnp.stack([k_r * g_i - k_i * g_r, v_r * g_i - v_i * g_r])
    conv = dft.inverse_real(prod_r, prod_i, lax.Precision.HIGH)
    conv_grad, kernel_grad = conv[0], conv[1]

    d_values = conv_grad.astype(jnp.bfloat16)
    d_gate = (grad_c * conv_out).astype(jnp.bfloat16)
    d_filt_c = kernel_grad * window * norm_scale
    decay_part = jnp.sum(position * kernel_grad * kernel, axis=(0, 2))

    back = to_tokens(jnp.stack([d_values, d_gate]), parts)
    lanes = 128
    slab = jnp.zeros((parts, sub, lanes), jnp.float32).at[:, :, 0].set(
        jnp.broadcast_to(decay_part[None, :], (parts, sub))
    )
    moved = lax.all_to_all(
        jnp.concatenate([d_filt_c, slab], axis=2), "seq", split_axis=0, concat_axis=0, tiled=True
    )
    d_filt = jnp.transpose(moved[:, :, :tok_rows].reshape(width, tok_rows))
    decay_grad = -norm_scale * moved[:, :, tok_rows].reshape(width)
    return (back[0], back[1], d_filt, decay_grad, d_out_weight)


def solution(mesh):
    in_specs = (
        P("seq", "tp"),
        P("seq", "tp"),
        P("seq", "tp"),
        P(None, "tp"),
        P("seq", "tp"),
        P("tp"),
    )
    out_specs = (P("seq", "tp"), P("seq", "tp"), P("seq", "tp"), P("tp"), P("seq", "tp"))
    return jax.shard_map(
        on_device, mesh=mesh, in_specs=in_specs, out_specs=out_specs, check_vma=False
    )
```
